32 devices in a mesh: group: 8 (over y, x, core), member: 4 (over z).
Axes of the slice: x: 2, y: 2, z: 4, core: 2. Of those that a mesh axis runs over, the one named last changes fastest.
Arguments:
- points: bfloat16 [49152, 128], P(('group', 'member')), may hold values from -3 to 3
- right_sides: float32 [49152, 256], P(('group', 'member')), may hold values from -6 to 6
- leaf_order: int32 [32, 1536], P(('group', 'member')), may hold values from 0 to 1535, each once within a row
- near_leaves: int32 [32, 2], P(('group', 'member')), may hold values from 0 to 3, as said below
- bases: bfloat16 [49152, 128], P(('group', 'member')), may hold values from -0.15625 to 0.15625
- couplings: bfloat16 [32, 4, 128, 128], P(('group', 'member')), may hold values from -0.25 to 0.25
- transfers: bfloat16 [32, 128, 128], P(('group', 'member')), may hold values from -0.5 to 0.5
- cross_couplings: bfloat16 [8, 8, 128, 128], P('group'), may hold values from -0.1875 to 0.1875
- low_bound: float32 [1], replicated, may hold values from 0.5 to 2.5
- high_bound: float32 [1], replicated, may hold values from 4 to 8
Outputs:
- solution: float32 [49152, 256], P(('group', 'member'))
- residual: float32 [49152, 256], P(('group', 'member'))
The draws below stay inside these ranges and needn't reach their ends.
Inputs may be any that keep to these rules, and one draw needn't show every extreme that they name: `near_leaves`: each leaf's two entries differ from each other and from the leaf's own member index, and lie within two member positions of it.
All inputs are finite; a program needn't handle non-finite values.
Results may differ from the reference program's by a relative error of at most 0.0085.
Values may be sent and summed in bfloat16 or wider, within the bound.
No kernel may reach another device: no remote copies, remote signals or barrier semaphores. Data moves between devices by JAX's collectives and lax.ppermute only.
A program may use at most 128 MiB of HBM per device.

```python
import jax
import jax.numpy as jnp
from jax import lax

LEAF = 1536
PT_DIM = 128
RANK = 128
NRHS = 256
GROUPS = 8
MEMBERS = 4
LEAVES = 32
POINTS = 49152


def draw_near_leaves(key, part):
    leaves = GROUPS * MEMBERS
    member_ids = jnp.arange(leaves, dtype=jnp.int32) % MEMBERS
    offsets = jnp.array([-2, -1, 1, 2], dtype=jnp.int32)
    candidate = member_ids[:, None] + offsets[None, :]
    valid = (candidate >= 0) & (candidate < MEMBERS)
    scores = jax.random.randint(jax.random.fold_in(key, 17), (leaves, 4), 0, 1000, dtype=jnp.int32) * 4
    scores = scores + jnp.arange(4, dtype=jnp.int32)[None, :]
    scores = jnp.where(valid, scores, -1)
    _, chosen = lax.top_k(scores, 2)
    return jnp.take_along_axis(candidate, chosen, axis=1).astype(jnp.int32)


def level_of(rng, dims, pieces, least, top_value):
    level = 1.0
    for axis_at, shards_of in pieces:
        heights = jax.random.uniform(jax.random.fold_in(jax.random.fold_in(rng, 6), axis_at), (shards_of,), jnp.float32, least / len(pieces), top_value / len(pieces))
        level = level * jnp.repeat(jnp.exp(heights), dims[axis_at] // shards_of).reshape((-1,) + (1,) * (len(dims) - 1 - axis_at))
    return level


def gaussian(key, extent, spread, reach, cuts=(), kind=jnp.bfloat16):
    drawn = jax.random.normal(key, extent, jnp.float32) * spread
    if len(cuts) > 0:
        drawn = level_of(key, extent, cuts, -0.22, 0.18) * drawn
    return jnp.clip(drawn, min=-reach, max=reach).astype(kind)


def setup_inputs(seed: int = 0) -> dict:
    keys = jax.random.split(jax.random.key(seed), 11)
    return {
        "points": gaussian(keys[0], (POINTS, PT_DIM), 0.5, 3.0, ((0, 32),)),
        "right_sides": gaussian(keys[1], (POINTS, NRHS), 1.0, 6.0, ((0, 32),), jnp.float32),
        "leaf_order": jax.vmap(lambda own: jax.random.permutation(own, LEAF))(jax.random.split(keys[2], LEAVES)).reshape((LEAVES, LEAF)).astype(jnp.int32),
        "near_leaves": draw_near_leaves(jax.random.fold_in(keys[10], 71), 0),
        "bases": gaussian(keys[4], (POINTS, RANK), LEAF ** -0.5, 0.15625, ((0, 32),)),
        "couplings": gaussian(keys[5], (LEAVES, MEMBERS, RANK, RANK), (RANK * MEMBERS) ** -0.5, 0.25, ((0, 32),)),
        "transfers": gaussian(keys[6], (LEAVES, RANK, RANK), (RANK * MEMBERS // 4) ** -0.5, 0.5, ((0, 32),)),
        "cross_couplings": gaussian(keys[7], (GROUPS, GROUPS, RANK, RANK), (RANK * GROUPS) ** -0.5, 0.1875, ((0, 8),)),
        "low_bound": jnp.clip(jax.random.uniform(keys[8], (1,), jnp.float32, 0.5, 2.5), 0.5, 2.5),
        "high_bound": jnp.clip(jax.random.uniform(keys[9], (1,), jnp.float32, 4.0, 8.0), 4.0, 8.0),
    }


RIDGE = 0.5
KERNEL_WIDTH = 8.0


def kernel_block(left, right):
    cross = jnp.dot(left, right.T, preferred_element_type=jnp.float32)
    left_squared_norm = jnp.sum(jnp.square(left.astype(jnp.float32)), axis=1)
    right_sq = jnp.sum(jnp.square(right.astype(jnp.float32)), axis=1)
    dist = left_squared_norm[:, None] + right_sq[None, :] - 2.0 * cross
    log_gain = left.shape[1] / 16.0
    return (jnp.exp(log_gain - dist / KERNEL_WIDTH) / (2.0 * LEAF)).astype(jnp.bfloat16)


def reference(points, right_sides, leaf_order, near_leaves, bases, couplings, transfers, cross_couplings, low_bound, high_bound):
    leaves = GROUPS * MEMBERS
    pts = points.reshape(leaves, LEAF, PT_DIM)
    basis = bases.reshape(leaves, LEAF, RANK).astype(jnp.float32)
    rhs = right_sides.reshape(leaves, LEAF, NRHS)
    ordered = jax.vmap(lambda rows, order: jnp.take(rows, order, axis=0))(rhs, leaf_order)
    leaf_ids = jnp.arange(leaves, dtype=jnp.int32)
    member_ids = leaf_ids % MEMBERS
    group_base = (leaf_ids // MEMBERS) * MEMBERS
    near_global = group_base[:, None] + near_leaves
    columns = jnp.arange(MEMBERS, dtype=jnp.int32)[None, :]
    far_mask = ((columns != member_ids[:, None]) & (columns != near_leaves[:, 0:1]) & (columns != near_leaves[:, 1:2])).astype(jnp.float32)
    masked = couplings.astype(jnp.float32) * far_mask[:, :, None, None]
    masked = masked.reshape(GROUPS, MEMBERS, MEMBERS, RANK, RANK)
    cross_mask = 1.0 - jnp.eye(GROUPS, dtype=jnp.float32)
    cross_masked = cross_couplings.astype(jnp.float32) * cross_mask[:, :, None, None]
    leaf_transfer_matrix = transfers.astype(jnp.float32)

    def apply_operator(direction):
        dir_bf = direction.astype(jnp.bfloat16)

        def near_one(leaf):
            own = pts[leaf]
            first = near_global[leaf, 0]
            second = near_global[leaf, 1]
            total = jnp.dot(kernel_block(own, own), dir_bf[leaf], preferred_element_type=jnp.float32)
            total = total + jnp.dot(kernel_block(own, pts[first]), dir_bf[first], preferred_element_type=jnp.float32)
            total = total + jnp.dot(kernel_block(own, pts[second]), dir_bf[second], preferred_element_type=jnp.float32)
            return total

        near = lax.map(near_one, leaf_ids)
        coeff = jnp.einsum('lpr,lpn->lrn', basis, dir_bf.astype(jnp.float32)).astype(jnp.bfloat16)
        leaf_coefficient_rows = coeff.astype(jnp.float32)
        within = jnp.einsum('gmjrs,gjsn->gmrn', masked, leaf_coefficient_rows.reshape(GROUPS, MEMBERS, RANK, NRHS))
        part = jnp.einsum('oqz,oqy->ozy', leaf_transfer_matrix, leaf_coefficient_rows)
        merged = jnp.sum(part.reshape(GROUPS, MEMBERS, RANK, NRHS), axis=1).astype(jnp.bfloat16)
        cross_product_result = jnp.einsum('ghrs,hsn->grn', cross_masked, merged.astype(jnp.float32)).astype(jnp.bfloat16)
        leaf_cross_product = jnp.repeat(cross_product_result.astype(jnp.float32), MEMBERS, axis=0)
        lifted = jnp.einsum('lrs,lsn->lrn', leaf_transfer_matrix, leaf_cross_product)
        coupled = (within.reshape(leaves, RANK, NRHS) + lifted).astype(jnp.bfloat16)
        far = jnp.einsum('lpr,lrn->lpn', basis, coupled.astype(jnp.float32))
        return RIDGE * direction + near + far

    lower = low_bound[0]
    upper = high_bound[0]
    theta = (upper + lower) / 2.0
    delta = (upper - lower) / 2.0
    sigma = theta / delta
    rho_zero = 1.0 / sigma
    rho_one = 1.0 / (2.0 * sigma - rho_zero)
    step_zero = ordered / theta
    initial_residual = ordered - apply_operator(step_zero)
    step_one = rho_one * rho_zero * step_zero + (2.0 * rho_one / delta) * initial_residual
    solution = step_zero + step_one
    second_res = initial_residual - apply_operator(step_one)
    return solution.reshape(-1, NRHS), second_res.reshape(-1, NRHS)
```

```python
import functools
import math

import jax
import jax.numpy as jnp
from jax import lax
from jax.experimental import pallas as pl
from jax.experimental.pallas import tpu as pltpu
from jax.sharding import PartitionSpec as P

RIDGE = 0.5
KERNEL_WIDTH = 8.0
REACH = 2
F32 = jnp.float32
BF16 = jnp.bfloat16
VMEM = pltpu.VMEM
ANY = pl.ANY


def shift(array, axis, by):
    count = lax.axis_size(axis)
    pairs = [(i, i + by) for i in range(count) if 0 <= i + by < count]
    return lax.ppermute(array, axis, pairs)


def cycle(array, axis, by):
    count = lax.axis_size(axis)
    return lax.ppermute(array, axis, [(i, (i + by) % count) for i in range(count)])


def tile_of(rows):
    return 256 if rows % 256 == 0 else rows


def whole(array):
    dims = array.ndim
    return pl.BlockSpec(array.shape, lambda *_: (0,) * dims)


def by_rows(tile, width):
    return pl.BlockSpec((tile, width), lambda i: (i, 0))


SMEM_SPEC = pl.BlockSpec(memory_space=pltpu.SMEM)
ANY_SPEC = pl.BlockSpec(memory_space=ANY)


def call(body, name, out, args, in_specs, out_specs, grid=(), scratch=(), flops=0, bytes_=0, exps=0):
    return pl.pallas_call(
        body,
        name=name,
        out_shape=out,
        grid=grid,
        in_specs=in_specs,
        out_specs=out_specs,
        scratch_shapes=list(scratch),
        cost_estimate=pl.CostEstimate(flops=flops, bytes_accessed=bytes_, transcendentals=exps),
        compiler_params=pltpu.CompilerParams(vmem_limit_bytes=40 * 1024 * 1024),
    )(*args)


def dot(left, right):
    return jnp.dot(left, right, preferred_element_type=F32)


def dot_tn(left, right):
    return lax.dot_general(left, right, (((0,), (0,)), ((), ())), preferred_element_type=F32)


def dot_nt(left, right):
    return lax.dot_general(left, right, (((1,), (1,)), ((), ())), preferred_element_type=F32)


def pieces(value):
    first = value.astype(BF16).astype(F32)
    rest = value - first
    second = rest.astype(BF16).astype(F32)
    return first, second, rest - second


def augmented(block, left):
    rows, dims = block.shape
    wide = block.astype(F32)
    norm = jnp.sum(wide * wide, axis=1, keepdims=True)
    value = -norm / KERNEL_WIDTH
    if left:
        value = value + (dims / 16.0 - math.log(2.0 * rows))
        block = (wide * (2.0 / KERNEL_WIDTH)).astype(BF16)
    lane = lax.broadcasted_iota(jnp.int32, (rows, 128), 1)
    at, ones_at = (0, 3) if left else (3, 0)
    extra = jnp.where((lane >= ones_at) & (lane < ones_at + 3), 1.0, 0.0)
    for k, piece in enumerate(pieces(value)):
        extra = jnp.where(lane == at + k, piece, extra)
    return block, extra.astype(BF16)


def fill_augmented(target, block, left):
    dims = block.shape[1]
    main, extra = augmented(block, left)
    target[:, :dims] = main
    target[:, dims:] = extra


def kernel_tile(left_tile, right_all):
    return jnp.exp(dot_nt(left_tile, right_all)).astype(BF16)


def pick(choice, candidates, target, sem):
    for k, ref in enumerate(candidates):
        @pl.when(choice == k)
        def _():
            copy = pltpu.make_async_copy(ref, target, sem)
            copy.start()
            copy.wait()


def slots(near_ref, members):
    member = lax.axis_index("member")
    one = near_ref[0, 0] - member
    two = near_ref[0, 1] - member
    if members <= 2 * REACH:
        before = (one == -1) | (two == -1)
        after = (one == 1) | (two == 1)
        behind = (one == -2) | (two == -2)
        slot_a = jnp.where(before, 0, 1)
        slot_b = jnp.where(before & after, 0, jnp.where(behind, 1, 2))
        return slot_a, slot_b

    def index(offset):
        return jnp.where(offset == -1, 0, jnp.where(offset == 1, 1, jnp.where(offset == -2, 2, 3)))

    return index(one), index(two)


def slot_candidates(moved, members):
    before, after, behind, ahead = moved
    if members <= 2 * REACH:
        return (before, after), (after, behind, ahead)
    return moved, moved


def factors(low_ref, high_ref, width):
    low = jnp.full((1, width), low_ref[0], F32)
    high = jnp.full((1, width), high_ref[0], F32)
    theta = (high + low) / 2.0
    delta = (high - low) / 2.0
    sigma = theta / delta
    rho_zero = 1.0 / sigma
    rho_one = 1.0 / (2.0 * sigma - rho_zero)
    return theta, rho_one * rho_zero, 2.0 * rho_one / delta


def prep(ordered, bases, transfer, low, high):
    rows, width = ordered.shape
    rank = bases.shape[1]
    tile = tile_of(rows)

    def body(low_ref, high_ref, ordered_ref, bases_ref, transfer_ref, v_ref, message_ref, total):
        step = pl.program_id(0)
        theta, _, _ = factors(low_ref, high_ref, width)
        v = (ordered_ref[...] / theta).astype(BF16)
        v_ref[...] = v
        part = dot_tn(bases_ref[...], v)

        @pl.when(step == 0)
        def _():
            total[...] = part

        @pl.when(step > 0)
        def _():
            total[...] += part

        @pl.when(step == pl.num_programs(0) - 1)
        def _():
            message_ref[:, :width] = total[...].astype(BF16)
            message_ref[:, width:] = transfer_ref[...]

    return call(
        body, "prep",
        (jax.ShapeDtypeStruct((rows, width), BF16), jax.ShapeDtypeStruct((rank, width + rank), BF16)),
        (low, high, ordered, bases, transfer),
        [SMEM_SPEC, SMEM_SPEC, by_rows(tile, width), by_rows(tile, rank), whole(transfer)],
        (by_rows(tile, width), pl.BlockSpec((rank, width + rank), lambda i: (0, 0))),
        grid=(rows // tile,), scratch=[VMEM((rank, width), F32)],
        flops=2 * rows * width * rank, bytes_=rows * width * 6 + rows * rank * 2,
    )


def self_first(points, ordered, v, low, high):
    rows, width = ordered.shape
    dims = points.shape[1]
    tile = tile_of(rows)

    def body(low_ref, high_ref, points_ref, ordered_ref, v_ref, block_ref, rest_ref, left, right):
        step = pl.program_id(0)

        @pl.when(step == 0)
        def _():
            fill_augmented(left, points_ref[...], True)
            fill_augmented(right, points_ref[...], False)

        theta, _, _ = factors(low_ref, high_ref, width)
        block = kernel_tile(left[pl.ds(step * tile, tile), :], right[...])
        block_ref[...] = block
        own = ordered_ref[...]
        rest_ref[...] = own - RIDGE * (own / theta) - dot(block, v_ref[...])

    return call(
        body, "self_first",
        (jax.ShapeDtypeStruct((rows, rows), BF16), jax.ShapeDtypeStruct((rows, width), F32)),
        (low, high, points, ordered, v),
        [SMEM_SPEC, SMEM_SPEC, whole(points), by_rows(tile, width), whole(v)],
        (by_rows(tile, rows), by_rows(tile, width)),
        grid=(rows // tile,),
        scratch=[VMEM((rows, dims + 128), BF16), VMEM((rows, dims + 128), BF16)],
        flops=2 * rows * rows * (width + dims), bytes_=rows * rows * 2 + rows * width * 10,
        exps=rows * rows,
    )


def near_block(name, which, near, points, candidates):
    rows, dims = points.shape
    members = lax.axis_size("member")
    tile = tile_of(rows)
    count = len(candidates)

    def body(near_ref, points_ref, *rest):
        others, (block_ref, other, left, right, sem) = rest[:count], rest[count:]
        step = pl.program_id(0)

        @pl.when(step == 0)
        def _():
            pick(slots(near_ref, members)[which], others, other, sem)
            fill_augmented(left, points_ref[...], True)
            fill_augmented(right, other[...], False)

        block_ref[...] = kernel_tile(left[pl.ds(step * tile, tile), :], right[...])

    return call(
        body, name,
        jax.ShapeDtypeStruct((rows, rows), BF16),
        (near, points, *candidates),
        [SMEM_SPEC, whole(points)] + [ANY_SPEC] * count,
        by_rows(tile, rows),
        grid=(rows // tile,),
        scratch=[VMEM((rows, dims), BF16), VMEM((rows, dims + 128), BF16),
                 VMEM((rows, dims + 128), BF16), pltpu.SemaphoreType.DMA],
        flops=2 * rows * rows * dims, bytes_=rows * rows * 2 + rows * dims * 4, exps=rows * rows,
    )


def subtract_near(name, which, near, block, rest, candidates):
    rows, width = rest.shape
    members = lax.axis_size("member")
    tile = tile_of(rows)
    count = len(candidates)

    def body(near_ref, block_ref, rest_ref, *refs):
        others, (out_ref, v, sem) = refs[:count], refs[count:]

        @pl.when(pl.program_id(0) == 0)
        def _():
            pick(slots(near_ref, members)[which], others, v, sem)

        out_ref[...] = rest_ref[...] - dot(block_ref[...], v[...])

    return call(
        body, name,
        jax.ShapeDtypeStruct((rows, width), F32),
        (near, block, rest, *candidates),
        [SMEM_SPEC, by_rows(tile, rows), by_rows(tile, width)] + [ANY_SPEC] * count,
        by_rows(tile, width),
        grid=(rows // tile,),
        scratch=[VMEM((rows, width), BF16), pltpu.SemaphoreType.DMA],
        flops=2 * rows * rows * width, bytes_=rows * rows * 2 + rows * width * 10,
    )


def turn(near, block, rest, candidates, bases, coupled, ordered, low, high):
    rows, width = rest.shape
    rank = bases.shape[1]
    members = lax.axis_size("member")
    tile = tile_of(rows)
    count = len(candidates)

    def body(low_ref, high_ref, near_ref, block_ref, rest_ref, bases_ref, coupled_ref, ordered_ref, *refs):
        others, (first_ref, v_ref, coeff_ref, v, total, sem) = refs[:count], refs[count:]
        step = pl.program_id(0)

        @pl.when(step == 0)
        def _():
            pick(slots(near_ref, members)[1], others, v, sem)

        theta, keep, push = factors(low_ref, high_ref, width)
        own = bases_ref[...]
        first = rest_ref[...] - dot(block_ref[...], v[...]) - dot(own, coupled_ref[...])
        first_ref[...] = first
        moved = (keep * (ordered_ref[...] / theta) + push * first).astype(BF16)
        v_ref[...] = moved
        part = dot_tn(own, moved)

        @pl.when(step == 0)
        def _():
            total[...] = part

        @pl.when(step > 0)
        def _():
            total[...] += part

        @pl.when(step == pl.num_programs(0) - 1)
        def _():
            coeff_ref[...] = total[...].astype(BF16)

    return call(
        body, "turn",
        (jax.ShapeDtypeStruct((rows, width), F32), jax.ShapeDtypeStruct((rows, width), BF16),
         jax.ShapeDtypeStruct((rank, width), BF16)),
        (low, high, near, block, rest, bases, coupled, ordered, *candidates),
        [SMEM_SPEC, SMEM_SPEC, SMEM_SPEC, by_rows(tile, rows), by_rows(tile, width), by_rows(tile, rank),
         whole(coupled), by_rows(tile, width)] + [ANY_SPEC] * count,
        (by_rows(tile, width), by_rows(tile, width), pl.BlockSpec((rank, width), lambda i: (0, 0))),
        grid=(rows // tile,),
        scratch=[VMEM((rows, width), BF16), VMEM((rank, width), F32), pltpu.SemaphoreType.DMA],
        flops=2 * rows * rows * width, bytes_=rows * rows * 2 + rows * width * 16,
    )


def self_second(block, v, first, ordered, low, high):
    rows, width = first.shape
    tile = tile_of(rows)

    def body(low_ref, high_ref, block_ref, v_ref, first_ref, ordered_ref, solution_ref, rest_ref):
        theta, keep, push = factors(low_ref, high_ref, width)
        first = first_ref[...]
        step_zero = ordered_ref[...] / theta
        step_one = keep * step_zero + push * first
        solution_ref[...] = step_zero + step_one
        rest_ref[...] = first - RIDGE * step_one - dot(block_ref[...], v_ref[...])

    return call(
        body, "self_second",
        (jax.ShapeDtypeStruct((rows, width), F32), jax.ShapeDtypeStruct((rows, width), F32)),
        (low, high, block, v, first, ordered),
        [SMEM_SPEC, SMEM_SPEC, by_rows(tile, rows), whole(v), by_rows(tile, width), by_rows(tile, width)],
        (by_rows(tile, width), by_rows(tile, width)),
        grid=(rows // tile,),
        flops=2 * rows * rows * width, bytes_=rows * rows * 2 + rows * width * 18,
    )


def final(near, block, rest, candidates, bases, coupled):
    rows, width = rest.shape
    rank = bases.shape[1]
    members = lax.axis_size("member")
    tile = tile_of(rows)
    count = len(candidates)

    def body(near_ref, block_ref, rest_ref, bases_ref, coupled_ref, *refs):
        others, (out_ref, v, sem) = refs[:count], refs[count:]

        @pl.when(pl.program_id(0) == 0)
        def _():
            pick(slots(near_ref, members)[1], others, v, sem)

        out_ref[...] = rest_ref[...] - dot(block_ref[...], v[...]) - dot(bases_ref[...], coupled_ref[...])

    return call(
        body, "final",
        jax.ShapeDtypeStruct((rows, width), F32),
        (near, block, rest, bases, coupled, *candidates),
        [SMEM_SPEC, by_rows(tile, rows), by_rows(tile, width), by_rows(tile, rank), whole(coupled)]
        + [ANY_SPEC] * count,
        by_rows(tile, width),
        grid=(rows // tile,),
        scratch=[VMEM((rows, width), BF16), pltpu.SemaphoreType.DMA],
        flops=2 * rows * rows * width, bytes_=rows * rows * 2 + rows * width * 10,
    )


def merge(name, own, messages, first_own, first_messages):
    rank = own.shape[0]
    width = first_own.shape[1] - rank
    count = len(messages)

    def body(*refs):
        coeffs, firsts, out_ref = refs[: count + 1], refs[count + 1 : 2 * count + 2], refs[-1]
        total = None
        for coeff, carried in zip(coeffs, firsts):
            part = dot_tn(carried[:, width:], coeff[:, :width])
            total = part if total is None else total + part
        out_ref[...] = total.astype(BF16)

    args = (own, *messages, first_own, *first_messages)
    return call(
        body, name, jax.ShapeDtypeStruct((rank, width), BF16), args,
        [whole(a) for a in args], pl.BlockSpec((rank, width), lambda: (0, 0)),
        flops=2 * rank * rank * width * (count + 1), bytes_=rank * width * 2 * (2 * count + 3),
    )


def couple(name, near, couplings, transfer, cross, messages, merged):
    rank = transfer.shape[0]
    width = merged[0].shape[1]
    members = lax.axis_size("member")
    groups = lax.axis_size("group")

    def body(near_ref, couplings_ref, transfer_ref, cross_ref, *refs):
        coeffs, others, out_ref = refs[: members - 1], refs[members - 1 : -1], refs[-1]
        member = lax.axis_index("member")
        group = lax.axis_index("group")
        crossed = jnp.zeros((rank, width), F32)
        for k, other in enumerate(others):
            source = lax.rem(group + (groups - 1 - k), groups)
            crossed = crossed + dot(cross_ref[source], other[...])
        within = dot(transfer_ref[...], crossed.astype(BF16))
        for k, coeff in enumerate(coeffs):
            source = lax.rem(member + (members - 1 - k), members)
            far = (source != near_ref[0, 0]) & (source != near_ref[0, 1])
            within = within + jnp.where(far, 1.0, 0.0) * dot(couplings_ref[source], coeff[:, :width])
        out_ref[...] = within.astype(BF16)

    args = (near, couplings, transfer, cross, *messages, *merged)
    return call(
        body, name, jax.ShapeDtypeStruct((rank, width), BF16), args,
        [SMEM_SPEC] + [whole(a) for a in args[1:]], pl.BlockSpec((rank, width), lambda: (0, 0)),
        flops=2 * rank * rank * width * (members + groups), bytes_=rank * width * 2 * (members + groups) * 2,
    )


def around(array, axis):
    return [cycle(array, axis, k) for k in range(1, lax.axis_size(axis))]


def exchange(block):
    before = shift(block, "member", 1)
    after = shift(block, "member", -1)
    behind = shift(before, "member", 1)
    ahead = shift(after, "member", -1)
    return before, after, behind, ahead


def shards(
    points,
    right_sides,
    leaf_order,
    near_leaves,
    bases,
    couplings,
    transfers,
    cross_couplings,
    low_bound,
    high_bound,
):
    members = lax.axis_size("member")
    transfer = transfers[0]
    couplings = couplings[0]
    cross = cross_couplings[0]
    near = near_leaves
    low, high = low_bound, high_bound

    with jax.named_scope("points"):
        points_moved = exchange(points)
    points_a, points_b = slot_candidates(points_moved, members)
    ordered = right_sides.at[leaf_order[0]].get(mode="promise_in_bounds", unique_indices=True)
    v0, message = prep(ordered, bases, transfer, low, high)
    with jax.named_scope("message_first"):
        messages = around(message, "member")
    with jax.named_scope("rows_first"):
        v0_a, v0_b = slot_candidates(exchange(v0), members)
    own_block, rest = self_first(points, ordered, v0, low, high)
    merged = merge("merge_first", message, messages, message, messages)
    with jax.named_scope("merged_first"):
        merged_all = around(merged, "group")
    coupled = couple("couple_first", near, couplings, transfer, cross, messages, merged_all)
    block_a = near_block("block_a", 0, near, points, points_a)
    rest = subtract_near("near_first", 0, near, block_a, rest, v0_a)
    block_b = near_block("block_b", 1, near, points, points_b)
    first, v1, coeff = turn(near, block_b, rest, v0_b, bases, coupled, ordered, low, high)

    with jax.named_scope("message_second"):
        coeffs = around(coeff, "member")
    with jax.named_scope("rows_second"):
        v1_a, v1_b = slot_candidates(exchange(v1), members)
    solution_rows, rest = self_second(own_block, v1, first, ordered, low, high)
    merged = merge("merge_second", coeff, coeffs, message, messages)
    with jax.named_scope("merged_second"):
        merged_all = around(merged, "group")
    coupled = couple("couple_second", near, couplings, transfer, cross, coeffs, merged_all)
    rest = subtract_near("near_second", 0, near, block_a, rest, v1_a)
    residual = final(near, block_b, rest, v1_b, bases, coupled)
    return solution_rows, residual


def solution(mesh):
    return jax.shard_map(
        shards,
        mesh=mesh,
        in_specs=(
            P(("group", "member"), None),
            P(("group", "member"), None),
            P(("group", "member"), None),
            P(("group", "member"), None),
            P(("group", "member"), None),
            P(("group", "member"), None, None, None),
            P(("group", "member"), None, None),
            P("group", None, None, None),
            P(),
            P(),
        ),
        out_specs=(P(("group", "member"), None), P(("group", "member"), None)),
        check_vma=False,
    )
```

```python
import math

import jax
import jax.numpy as jnp
from jax import lax
from jax.experimental import pallas as pl
from jax.experimental.pallas import tpu as pltpu
from jax.sharding import PartitionSpec as P


RIDGE = 0.5
KERNEL_WIDTH = 8.0
REACH = 2
F32 = jnp.float32
BF16 = jnp.bfloat16
VMEM = pltpu.VMEM
ANY = pl.ANY


def shift(array, axis, by):
    count = lax.axis_size(axis)
    pairs = [(i, i + by) for i in range(count) if 0 <= i + by < count]
    return lax.ppermute(array, axis, pairs)


def cycle(array, axis, by):
    count = lax.axis_size(axis)
    return lax.ppermute(array, axis, [(i, (i + by) % count) for i in range(count)])


def tile_of(rows):
    return 256 if rows % 256 == 0 else rows


def whole(array):
    dims = array.ndim
    return pl.BlockSpec(array.shape, lambda *_: (0,) * dims)


def by_rows(tile, width):
    return pl.BlockSpec((tile, width), lambda i: (i, 0))


SMEM_SPEC = pl.BlockSpec(memory_space=pltpu.SMEM)
ANY_SPEC = pl.BlockSpec(memory_space=ANY)


def call(body, out, args, in_specs, out_specs, grid=(), scratch=(), flops=0, bytes_=0, exps=0):
    return pl.pallas_call(
        body,
        out_shape=out,
        grid=grid,
        in_specs=in_specs,
        out_specs=out_specs,
        scratch_shapes=list(scratch),
        cost_estimate=pl.CostEstimate(flops=flops, bytes_accessed=bytes_, transcendentals=exps),
        compiler_params=pltpu.CompilerParams(vmem_limit_bytes=16 * 1024 * 1024),
    )(*args)


def dot(left, right):
    return jnp.dot(left, right, preferred_element_type=F32)


def dot_tn(left, right):
    return lax.dot_general(left, right, (((0,), (0,)), ((), ())), preferred_element_type=F32)


def dot_nt(left, right):
    return lax.dot_general(left, right, (((1,), (1,)), ((), ())), preferred_element_type=F32)


def pieces(value):
    first = value.astype(BF16).astype(F32)
    rest = value - first
    second = rest.astype(BF16).astype(F32)
    return first, second, rest - second


def augmented(block, left):
    rows, dims = block.shape
    wide = block.astype(F32)
    norm = jnp.sum(wide * wide, axis=1, keepdims=True)
    value = -norm / KERNEL_WIDTH
    if left:
        value = value + (dims / 16.0 - math.log(2.0 * rows))
        block = (wide * (2.0 / KERNEL_WIDTH)).astype(BF16)
    lane = lax.broadcasted_iota(jnp.int32, (rows, 128), 1)
    at, ones_at = (0, 3) if left else (3, 0)
    extra = jnp.where((lane >= ones_at) & (lane < ones_at + 3), 1.0, 0.0)
    for k, piece in enumerate(pieces(value)):
        extra = jnp.where(lane == at + k, piece, extra)
    return block, extra.astype(BF16)


def fill_augmented(target, block, left):
    dims = block.shape[1]
    main, extra = augmented(block, left)
    target[:, :dims] = main
    target[:, dims:] = extra


def kernel_tile(left_tile, right_all):
    return jnp.exp(dot_nt(left_tile, right_all)).astype(BF16)


def pick(choice, candidates, target, sem):
    for k, ref in enumerate(candidates):
        @pl.when(choice == k)
        def _():
            copy = pltpu.make_async_copy(ref, target, sem)
            copy.start()
            copy.wait()


def slots(near_ref, members):
    member = lax.axis_index("member")
    one = near_ref[0, 0] - member
    two = near_ref[0, 1] - member
    if members <= 2 * REACH:
        before = (one == -1) | (two == -1)
        after = (one == 1) | (two == 1)
        behind = (one == -2) | (two == -2)
        slot_a = jnp.where(before, 0, 1)
        slot_b = jnp.where(before & after, 0, jnp.where(behind, 1, 2))
        return slot_a, slot_b

    def index(offset):
        return jnp.where(offset == -1, 0, jnp.where(offset == 1, 1, jnp.where(offset == -2, 2, 3)))

    return index(one), index(two)


def slot_candidates(moved, members):
    before, after, behind, ahead = moved
    if members <= 2 * REACH:
        return (before, after), (after, behind, ahead)
    return moved, moved


def factors(low_ref, high_ref, width):
    low = jnp.full((1, width), low_ref[0], F32)
    high = jnp.full((1, width), high_ref[0], F32)
    theta = (high + low) / 2.0
    delta = (high - low) / 2.0
    sigma = theta / delta
    rho_zero = 1.0 / sigma
    rho_one = 1.0 / (2.0 * sigma - rho_zero)
    return theta, rho_one * rho_zero, 2.0 * rho_one / delta


def prep(ordered, bases, transfer, low, high):
    rows, width = ordered.shape
    rank = bases.shape[1]
    tile = tile_of(rows)

    def body(low_ref, high_ref, ordered_ref, bases_ref, transfer_ref, v_ref, message_ref, total):
        step = pl.program_id(0)
        theta, _, _ = factors(low_ref, high_ref, width)
        v = (ordered_ref[...] / theta).astype(BF16)
        v_ref[...] = v
        part = dot_tn(bases_ref[...], v)

        @pl.when(step == 0)
        def _():
            total[...] = part

        @pl.when(step > 0)
        def _():
            total[...] += part

        @pl.when(step == pl.num_programs(0) - 1)
        def _():
            message_ref[:, :width] = total[...].astype(BF16)
            message_ref[:, width:] = transfer_ref[...]

    return call(
        body,
        (jax.ShapeDtypeStruct((rows, width), BF16), jax.ShapeDtypeStruct((rank, width + rank), BF16)),
        (low, high, ordered, bases, transfer),
        [SMEM_SPEC, SMEM_SPEC, by_rows(tile, width), by_rows(tile, rank), whole(transfer)],
        (by_rows(tile, width), pl.BlockSpec((rank, width + rank), lambda i: (0, 0))),
        grid=(rows // tile,), scratch=[VMEM((rank, width), F32)],
        flops=2 * rows * width * rank, bytes_=rows * width * 6 + rows * rank * 2,
    )


def self_first(points, ordered, v, low, high):
    rows, width = ordered.shape
    dims = points.shape[1]
    tile = tile_of(rows)

    def body(low_ref, high_ref, points_ref, ordered_ref, v_ref, block_ref, rest_ref, left, right):
        step = pl.program_id(0)

        @pl.when(step == 0)
        def _():
            fill_augmented(left, points_ref[...], True)
            fill_augmented(right, points_ref[...], False)

        theta, _, _ = factors(low_ref, high_ref, width)
        block = kernel_tile(left[pl.ds(step * tile, tile), :], right[...])
        block_ref[...] = block
        own = ordered_ref[...]
        rest_ref[...] = own - RIDGE * (own / theta) - dot(block, v_ref[...])

    return call(
        body,
        (jax.ShapeDtypeStruct((rows, rows), BF16), jax.ShapeDtypeStruct((rows, width), F32)),
        (low, high, points, ordered, v),
        [SMEM_SPEC, SMEM_SPEC, whole(points), by_rows(tile, width), whole(v)],
        (by_rows(tile, rows), by_rows(tile, width)),
        grid=(rows // tile,),
        scratch=[VMEM((rows, dims + 128), BF16), VMEM((rows, dims + 128), BF16)],
        flops=2 * rows * rows * (width + dims), bytes_=rows * rows * 2 + rows * width * 10,
        exps=rows * rows,
    )


def near_block(which, near, points, candidates):
    rows, dims = points.shape
    members = lax.axis_size("member")
    tile = tile_of(rows)
    count = len(candidates)

    def body(near_ref, points_ref, *rest):
        others, (block_ref, other, left, right, sem) = rest[:count], rest[count:]
        step = pl.program_id(0)

        @pl.when(step == 0)
        def _():
            pick(slots(near_ref, members)[which], others, other, sem)
            fill_augmented(left, points_ref[...], True)
            fill_augmented(right, other[...], False)

        block_ref[...] = kernel_tile(left[pl.ds(step * tile, tile), :], right[...])

    return call(
        body,
        jax.ShapeDtypeStruct((rows, rows), BF16),
        (near, points, *candidates),
        [SMEM_SPEC, whole(points)] + [ANY_SPEC] * count,
        by_rows(tile, rows),
        grid=(rows // tile,),
        scratch=[VMEM((rows, dims), BF16), VMEM((rows, dims + 128), BF16),
                 VMEM((rows, dims + 128), BF16), pltpu.SemaphoreType.DMA],
        flops=2 * rows * rows * dims, bytes_=rows * rows * 2 + rows * dims * 4, exps=rows * rows,
    )


def subtract_near(which, near, block, rest, candidates):
    rows, width = rest.shape
    members = lax.axis_size("member")
    tile = tile_of(rows)
    count = len(candidates)

    def body(near_ref, block_ref, rest_ref, *refs):
        others, (out_ref, v, sem) = refs[:count], refs[count:]

        @pl.when(pl.program_id(0) == 0)
        def _():
            pick(slots(near_ref, members)[which], others, v, sem)

        out_ref[...] = rest_ref[...] - dot(block_ref[...], v[...])

    return call(
        body,
        jax.ShapeDtypeStruct((rows, width), F32),
        (near, block, rest, *candidates),
        [SMEM_SPEC, by_rows(tile, rows), by_rows(tile, width)] + [ANY_SPEC] * count,
        by_rows(tile, width),
        grid=(rows // tile,),
        scratch=[VMEM((rows, width), BF16), pltpu.SemaphoreType.DMA],
        flops=2 * rows * rows * width, bytes_=rows * rows * 2 + rows * width * 10,
    )


def turn(near, block, rest, candidates, bases, coupled, ordered, low, high):
    rows, width = rest.shape
    rank = bases.shape[1]
    members = lax.axis_size("member")
    tile = tile_of(rows)
    count = len(candidates)

    def body(low_ref, high_ref, near_ref, block_ref, rest_ref, bases_ref, coupled_ref, ordered_ref, *refs):
        others, (first_ref, v_ref, coeff_ref, v, total, sem) = refs[:count], refs[count:]
        step = pl.program_id(0)

        @pl.when(step == 0)
        def _():
            pick(slots(near_ref, members)[1], others, v, sem)

        theta, keep, push = factors(low_ref, high_ref, width)
        own = bases_ref[...]
        first = rest_ref[...] - dot(block_ref[...], v[...]) - dot(own, coupled_ref[...])
        first_ref[...] = first
        moved = (keep * (ordered_ref[...] / theta) + push * first).astype(BF16)
        v_ref[...] = moved
        part = dot_tn(own, moved)

        @pl.when(step == 0)
        def _():
            total[...] = part

        @pl.when(step > 0)
        def _():
            total[...] += part

        @pl.when(step == pl.num_programs(0) - 1)
        def _():
            coeff_ref[...] = total[...].astype(BF16)

    return call(
        body,
        (jax.ShapeDtypeStruct((rows, width), F32), jax.ShapeDtypeStruct((rows, width), BF16),
         jax.ShapeDtypeStruct((rank, width), BF16)),
        (low, high, near, block, rest, bases, coupled, ordered, *candidates),
        [SMEM_SPEC, SMEM_SPEC, SMEM_SPEC, by_rows(tile, rows), by_rows(tile, width), by_rows(tile, rank),
         whole(coupled), by_rows(tile, width)] + [ANY_SPEC] * count,
        (by_rows(tile, width), by_rows(tile, width), pl.BlockSpec((rank, width), lambda i: (0, 0))),
        grid=(rows // tile,),
        scratch=[VMEM((rows, width), BF16), VMEM((rank, width), F32), pltpu.SemaphoreType.DMA],
        flops=2 * rows * rows * width, bytes_=rows * rows * 2 + rows * width * 16,
    )


def self_second(block, v, first, ordered, low, high):
    rows, width = first.shape
    tile = tile_of(rows)

    def body(low_ref, high_ref, block_ref, v_ref, first_ref, ordered_ref, solution_ref, rest_ref):
        theta, keep, push = factors(low_ref, high_ref, width)
        first = first_ref[...]
        step_zero = ordered_ref[...] / theta
        step_one = keep * step_zero + push * first
        solution_ref[...] = step_zero + step_one
        rest_ref[...] = first - RIDGE * step_one - dot(block_ref[...], v_ref[...])

    return call(
        body,
        (jax.ShapeDtypeStruct((rows, width), F32), jax.ShapeDtypeStruct((rows, width), F32)),
        (low, high, block, v, first, ordered),
        [SMEM_SPEC, SMEM_SPEC, by_rows(tile, rows), whole(v), by_rows(tile, width), by_rows(tile, width)],
        (by_rows(tile, width), by_rows(tile, width)),
        grid=(rows // tile,),
        flops=2 * rows * rows * width, bytes_=rows * rows * 2 + rows * width * 18,
    )


def final(near, block, rest, candidates, bases, coupled):
    rows, width = rest.shape
    rank = bases.shape[1]
    members = lax.axis_size("member")
    tile = tile_of(rows)
    count = len(candidates)

    def body(near_ref, block_ref, rest_ref, bases_ref, coupled_ref, *refs):
        others, (out_ref, v, sem) = refs[:count], refs[count:]

        @pl.when(pl.program_id(0) == 0)
        def _():
            pick(slots(near_ref, members)[1], others, v, sem)

        out_ref[...] = rest_ref[...] - dot(block_ref[...], v[...]) - dot(bases_ref[...], coupled_ref[...])

    return call(
        body,
        jax.ShapeDtypeStruct((rows, width), F32),
        (near, block, rest, bases, coupled, *candidates),
        [SMEM_SPEC, by_rows(tile, rows), by_rows(tile, width), by_rows(tile, rank), whole(coupled)]
        + [ANY_SPEC] * count,
        by_rows(tile, width),
        grid=(rows // tile,),
        scratch=[VMEM((rows, width), BF16), pltpu.SemaphoreType.DMA],
        flops=2 * rows * rows * width, bytes_=rows * rows * 2 + rows * width * 10,
    )


def merge(own, messages, first_own, first_messages):
    rank = own.shape[0]
    width = first_own.shape[1] - rank
    count = len(messages)

    def body(*refs):
        coeffs, firsts, out_ref = refs[: count + 1], refs[count + 1 : 2 * count + 2], refs[-1]
        total = None
        for coeff, carried in zip(coeffs, firsts):
            part = dot_tn(carried[:, width:], coeff[:, :width])
            total = part if total is None else total + part
        out_ref[...] = total.astype(BF16)

    args = (own, *messages, first_own, *first_messages)
    return call(
        body, jax.ShapeDtypeStruct((rank, width), BF16), args,
        [whole(a) for a in args], pl.BlockSpec((rank, width), lambda: (0, 0)),
        flops=2 * rank * rank * width * (count + 1), bytes_=rank * width * 2 * (2 * count + 3),
    )


def couple(near, couplings, transfer, cross, messages, merged):
    rank = transfer.shape[0]
    width = merged[0].shape[1]
    members = lax.axis_size("member")
    groups = lax.axis_size("group")

    def body(near_ref, couplings_ref, transfer_ref, cross_ref, *refs):
        coeffs, others, out_ref = refs[: members - 1], refs[members - 1 : -1], refs[-1]
        member = lax.axis_index("member")
        group = lax.axis_index("group")
        crossed = jnp.zeros((rank, width), F32)
        for k, other in enumerate(others):
            source = lax.rem(group + (groups - 1 - k), groups)
            crossed = crossed + dot(cross_ref[source], other[...])
        within = dot(transfer_ref[...], crossed.astype(BF16))
        for k, coeff in enumerate(coeffs):
            source = lax.rem(member + (members - 1 - k), members)
            far = (source != near_ref[0, 0]) & (source != near_ref[0, 1])
            within = within + jnp.where(far, 1.0, 0.0) * dot(couplings_ref[source], coeff[:, :width])
        out_ref[...] = within.astype(BF16)

    args = (near, couplings, transfer, cross, *messages, *merged)
    return call(
        body, jax.ShapeDtypeStruct((rank, width), BF16), args,
        [SMEM_SPEC] + [whole(a) for a in args[1:]], pl.BlockSpec((rank, width), lambda: (0, 0)),
        flops=2 * rank * rank * width * (members + groups), bytes_=rank * width * 2 * (members + groups) * 2,
    )


def around(array, axis):
    moved = []
    for k in range(1, lax.axis_size(axis)):
        moved.append(cycle(array, axis, k))
    return moved


def exchange(block):
    before = shift(block, "member", 1)
    after = shift(block, "member", -1)
    behind = shift(before, "member", 1)
    ahead = shift(after, "member", -1)
    return before, after, behind, ahead


def shards(
    points,
    right_sides,
    leaf_order,
    near_leaves,
    bases,
    couplings,
    transfers,
    cross_couplings,
    low_bound,
    high_bound,
):
    members = lax.axis_size("member")
    transfer = transfers[0]
    couplings = couplings[0]
    cross = cross_couplings[0]
    near = near_leaves
    low, high = low_bound, high_bound

    points_moved = exchange(points)
    points_a, points_b = slot_candidates(points_moved, members)
    ordered = right_sides.at[leaf_order[0]].get(mode="promise_in_bounds", unique_indices=True)
    v0, message = prep(ordered, bases, transfer, low, high)
    messages = around(message, "member")
    v0_a, v0_b = slot_candidates(exchange(v0), members)
    own_block, rest = self_first(points, ordered, v0, low, high)
    merged = merge(message, messages, message, messages)
    merged_all = around(merged, "group")
    coupled = couple(near, couplings, transfer, cross, messages, merged_all)
    block_a = near_block(0, near, points, points_a)
    rest = subtract_near(0, near, block_a, rest, v0_a)
    block_b = near_block(1, near, points, points_b)
    first, v1, coeff = turn(near, block_b, rest, v0_b, bases, coupled, ordered, low, high)

    coeffs = around(coeff, "member")
    v1_a, v1_b = slot_candidates(exchange(v1), members)
    solution_rows, rest = self_second(own_block, v1, first, ordered, low, high)
    merged = merge(coeff, coeffs, message, messages)
    merged_all = around(merged, "group")
    coupled = couple(near, couplings, transfer, cross, coeffs, merged_all)
    rest = subtract_near(0, near, block_a, rest, v1_a)
    residual = final(near, block_b, rest, v1_b, bases, coupled)
    return solution_rows, residual


def solution(mesh):
    return jax.shard_map(
        shards,
        mesh=mesh,
        in_specs=(
            P(("group", "member"), None),
            P(("group", "member"), None),
            P(("group", "member"), None),
            P(("group", "member"), None),
            P(("group", "member"), None),
            P(("group", "member"), None, None, None),
            P(("group", "member"), None, None),
            P("group", None, None, None),
            P(),
            P(),
        ),
        out_specs=(P(("group", "member"), None), P(("group", "member"), None)),
        check_vma=False,
    )
```

```python
import functools
import math

import jax
import jax.numpy as jnp
from jax import lax
from jax.experimental import pallas as pl
from jax.experimental.pallas import tpu as pltpu
from jax.sharding import PartitionSpec as P


RIDGE = 0.5
KERNEL_WIDTH = 8.0
REACH = 2
F32 = jnp.float32
BF16 = jnp.bfloat16
VMEM = pltpu.VMEM
ANY = pl.ANY


def shift(array, axis, by):
    count = lax.axis_size(axis)
    pairs = [(i, i + by) for i in range(count) if 0 <= i + by < count]
    return lax.ppermute(array, axis, pairs)


def cycle(array, axis, by):
    count = lax.axis_size(axis)
    return lax.ppermute(array, axis, [(i, (i + by) % count) for i in range(count)])


def tile_of(rows):
    return 512 if rows % 512 == 0 else rows


def over_tiles(rows, body):
    tile = tile_of(rows)

    def step(k, carry):
        body(pl.ds(pl.multiple_of(k * tile, tile), tile))
        return carry

    lax.fori_loop(0, rows // tile, step, 0)


def shape(dtype, *dims):
    return jax.ShapeDtypeStruct(dims, dtype)


SMEM_SPEC = pl.BlockSpec(memory_space=pltpu.SMEM)
ANY_SPEC = pl.BlockSpec(memory_space=ANY)


VMEM_SPEC = pl.BlockSpec(memory_space=VMEM)
HBM_SPEC = pl.BlockSpec(memory_space=pltpu.HBM)


def call(body, out, args, scratch=(), scalars=0, in_specs=None, out_specs=None, flops=0, bytes_=0, exps=0,
         aliases=None):
    many = isinstance(out, tuple)
    return pl.pallas_call(
        body,
        out_shape=out,
        in_specs=in_specs or [SMEM_SPEC] * scalars + [VMEM_SPEC] * (len(args) - scalars),
        out_specs=out_specs or ((VMEM_SPEC,) * len(out) if many else VMEM_SPEC),
        scratch_shapes=list(scratch),
        input_output_aliases=aliases or {},
        cost_estimate=pl.CostEstimate(flops=flops, bytes_accessed=bytes_, transcendentals=exps),
        compiler_params=pltpu.CompilerParams(vmem_limit_bytes=20 * 1024 * 1024),
    )(*args)


def dot(left, right):
    return jnp.dot(left, right, preferred_element_type=F32)


def dot_tn(left, right):
    return lax.dot_general(left, right, (((0,), (0,)), ((), ())), preferred_element_type=F32)


def dot_nt(left, right):
    return lax.dot_general(left, right, (((1,), (1,)), ((), ())), preferred_element_type=F32)


def pieces(value):
    first = value.astype(BF16).astype(F32)
    rest = value - first
    second = rest.astype(BF16).astype(F32)
    return first, second, rest - second


def augmented(block, left):
    rows, dims = block.shape
    wide = block.astype(F32)
    norm = jnp.sum(wide * wide, axis=1, keepdims=True)
    value = -norm / KERNEL_WIDTH
    if left:
        value = value + (dims / 16.0 - math.log(2.0 * rows))
        block = (wide * (2.0 / KERNEL_WIDTH)).astype(BF16)
    lane = lax.broadcasted_iota(jnp.int32, (rows, 128), 1)
    at, ones_at = (0, 3) if left else (3, 0)
    extra = jnp.where((lane >= ones_at) & (lane < ones_at + 3), 1.0, 0.0)
    for k, piece in enumerate(pieces(value)):
        extra = jnp.where(lane == at + k, piece, extra)
    return block, extra.astype(BF16)


def fill_augmented(target, block, left):
    dims = block.shape[1]
    main, extra = augmented(block, left)
    target[:, :dims] = main
    target[:, dims:] = extra


def kernel_tile(left_tile, right_all):
    return jnp.exp(dot_nt(left_tile, right_all)).astype(BF16)


def pick(choice, candidates, use):
    for k, candidate in enumerate(candidates):
        @pl.when(choice == k)
        def _():
            use(candidate)


def paired(members):
    return members == 2 * REACH


def slots(near_ref, members):
    member = lax.axis_index("member")
    one = near_ref[0, 0] - member
    two = near_ref[0, 1] - member
    if paired(members):
        toward = 1 - 2 * lax.rem(member, 2)
        outer = (one == toward) | (two == toward)
        inner = (one == -toward) | (two == -toward)
        return jnp.where(outer, 0, 1), jnp.where(outer & inner, 0, 1)

    def index(offset):
        return jnp.where(offset == -1, 0, jnp.where(offset == 1, 1, jnp.where(offset == -2, 2, 3)))

    return index(one), index(two)


def beside_pair(member, members):
    other = member - 1 if member % 2 == 0 else member + 1
    return other if 0 <= other < members else member


def exchange(block):
    members = lax.axis_size("member")
    if paired(members):
        beside = [beside_pair(i, members) for i in range(members)]
        across_of = [b + REACH if b + REACH < members else b - REACH for b in beside]
        inner = lax.ppermute(block, "member", list(enumerate(beside)))
        outer = lax.ppermute(block, "member", [(i, i + 1 - 2 * (i % 2)) for i in range(members)])
        across = lax.ppermute(inner, "member", list(enumerate(across_of)))
        return (outer, inner), (inner, across)
    before = shift(block, "member", 1)
    after = shift(block, "member", -1)
    behind = shift(before, "member", 1)
    ahead = shift(after, "member", -1)
    moved = (before, after, behind, ahead)
    return moved, moved


def factors(low_ref, high_ref, width):
    low = jnp.broadcast_to(low_ref[...], (1, width))
    high = jnp.broadcast_to(high_ref[...], (1, width))
    theta = (high + low) / 2.0
    delta = (high - low) / 2.0
    sigma = theta / delta
    rho_zero = 1.0 / sigma
    rho_one = 1.0 / (2.0 * sigma - rho_zero)
    return theta, rho_one * rho_zero, 2.0 * rho_one / delta


def prep(ordered, bases, transfer, low, high):
    rows, width = ordered.shape
    rank = bases.shape[1]
    half = width // 2

    def body(low_ref, high_ref, ordered_ref, bases_hbm, transfer_hbm, lead_ref, trail_ref, message_ref,
             bases_ref, transfer_ref, total, sems):
        copies = (pltpu.make_async_copy(bases_hbm, bases_ref, sems.at[0]),
                  pltpu.make_async_copy(transfer_hbm, transfer_ref, sems.at[1]))
        for copy in copies:
            copy.start()
        theta, _, _ = factors(low_ref, high_ref, width)
        total[...] = jnp.zeros_like(total)

        def scale(at):
            v = (ordered_ref[at, :] / theta).astype(BF16)
            lead_ref[at, :] = v[:, :half]
            trail_ref[at, :] = v[:, half:]

        over_tiles(rows, scale)
        for copy in copies:
            copy.wait()

        def project(at):
            own = bases_ref[at, :]
            total[:, :half] += dot_tn(own, lead_ref[at, :])
            total[:, half:] += dot_tn(own, trail_ref[at, :])

        over_tiles(rows, project)
        message_ref[:, :width] = total[...].astype(BF16)
        message_ref[:, width:] = transfer_ref[...]

    return call(
        body,
        (shape(BF16, rows, half), shape(BF16, rows, width - half), shape(BF16, rank, width + rank)),
        (low, high, ordered, pltpu.with_memory_space_constraint(bases, pltpu.HBM),
         pltpu.with_memory_space_constraint(transfer, pltpu.HBM)),
        in_specs=[VMEM_SPEC, VMEM_SPEC, VMEM_SPEC, HBM_SPEC, HBM_SPEC],
        scratch=[VMEM((rows, rank), BF16), VMEM((rank, rank), BF16), VMEM((rank, width), F32),
                 pltpu.SemaphoreType.DMA((2,))],
        flops=2 * rows * width * rank, bytes_=rows * width * 6 + rows * rank * 2,
    )


def join(lead_ref, trail_ref, target):
    half = trail_ref.shape[1]
    target[:, :half] = lead_ref[...]
    target[:, half:] = trail_ref[...]


def self_first(points, ordered, lead, trail, low, high):
    rows, width = ordered.shape
    dims = points.shape[1]

    def body(low_ref, high_ref, points_ref, ordered_ref, lead_ref, trail_ref, block_ref, rest_ref,
             left, right, v):
        theta, _, _ = factors(low_ref, high_ref, width)
        join(lead_ref, trail_ref, v)
        fill_augmented(left, points_ref[...], True)
        fill_augmented(right, points_ref[...], False)

        def tile(at):
            block = kernel_tile(left[at, :], right[...])
            block_ref[at, :] = block
            own = ordered_ref[at, :]
            rest_ref[at, :] = own - RIDGE * (own / theta) - dot(block, v[...])

        over_tiles(rows, tile)

    return call(
        body, (shape(BF16, rows, rows), shape(F32, rows, width)),
        (low, high, points, ordered, lead, trail),
        scratch=[VMEM((rows, dims + 128), BF16), VMEM((rows, dims + 128), BF16), VMEM((rows, width), BF16)],
        flops=2 * rows * rows * (width + dims), bytes_=rows * rows * 2 + rows * width * 10,
        exps=rows * rows,
    )


def near_block(which, near, points, candidates):
    rows, dims = points.shape
    members = lax.axis_size("member")
    count = len(candidates)

    def body(near_ref, points_ref, *rest):
        others, (block_ref, left, right) = rest[:count], rest[count:]
        fill_augmented(left, points_ref[...], True)
        pick(slots(near_ref, members)[which], others,
             lambda points_of: fill_augmented(right, points_of[...], False))

        def tile(at):
            block_ref[at, :] = kernel_tile(left[at, :], right[...])

        over_tiles(rows, tile)

    return call(
        body, shape(BF16, rows, rows), (near, points, *candidates), scalars=1,
        scratch=[VMEM((rows, dims + 128), BF16), VMEM((rows, dims + 128), BF16)],
        flops=2 * rows * rows * dims, bytes_=rows * rows * 2 + rows * dims * 4, exps=rows * rows,
    )


def subtract_near(near, block, rest, leads, trails):
    rows, width = rest.shape
    members = lax.axis_size("member")
    count = len(leads)

    def body(near_ref, block_ref, rest_ref, *refs):
        pairs = list(zip(refs[:count], refs[count : 2 * count]))
        out_ref, v = refs[2 * count :]
        pick(slots(near_ref, members)[0], pairs, lambda pair: join(*pair, v))

        def tile(at):
            out_ref[at, :] = rest_ref[at, :] - dot(block_ref[at, :], v[...])

        over_tiles(rows, tile)

    return call(
        body, shape(F32, rows, width), (near, block, rest, *leads, *trails), scalars=1,
        scratch=[VMEM((rows, width), BF16)],
        flops=2 * rows * rows * width, bytes_=rows * rows * 2 + rows * width * 10,
    )


def turn(column, near, block, rest, candidates, bases, coupled, ordered, low, high, joined=()):
    rows, width = rest.shape
    rank = bases.shape[1]
    half = width // 2
    members = lax.axis_size("member")
    count = len(candidates)
    kept = len(joined)
    columns = slice(column * half, (column + 1) * half)

    def body(near_ref, low_ref, high_ref, block_ref, rest_ref, bases_ref, coupled_ref, ordered_ref, *refs):
        others, joined_refs = refs[:count], refs[count : count + kept]
        first_ref, v_ref, coeff_ref, v, total = refs[count + kept :]

        def copy(ref):
            v[...] = ref[...]

        pick(slots(near_ref, members)[1], others, copy)
        theta, keep, push = factors(low_ref, high_ref, half)
        total[...] = jnp.zeros_like(total)

        def tile(at):
            own = bases_ref[at, :]
            first = rest_ref[at, columns] - dot(block_ref[at, :], v[...]) - dot(own, coupled_ref[:, columns])
            first_ref[at, :] = first
            moved = (keep * (ordered_ref[at, columns] / theta) + push * first).astype(BF16)
            v_ref[at, :] = moved
            total[...] += dot_tn(own, moved)

        over_tiles(rows, tile)
        for joined_ref in joined_refs:
            coeff_ref[:, :half] = joined_ref[...]
        coeff_ref[:, kept * half :] = total[...].astype(BF16)

    return call(
        body,
        (shape(F32, rows, half), shape(BF16, rows, half), shape(BF16, rank, half * (kept + 1))),
        (near, low, high, block, rest, bases, coupled, ordered, *candidates, *joined), scalars=1,
        scratch=[VMEM((rows, half), BF16), VMEM((rank, half), F32)],
        flops=2 * rows * rows * half, bytes_=rows * rows * 2 + rows * half * 16,
    )


def self_second(block, lead, trail, first_lead, first_trail, ordered, low, high):
    rows, width = ordered.shape
    half = width // 2

    def body(low_ref, high_ref, block_ref, lead_ref, trail_ref, first_lead_ref, first_trail_ref, ordered_ref,
             solution_ref, rest_ref, v):
        join(lead_ref, trail_ref, v)
        theta, keep, push = factors(low_ref, high_ref, half)

        def tile(at):
            product = dot(block_ref[at, :], v[...])
            for k, ref in enumerate((first_lead_ref, first_trail_ref)):
                columns = slice(k * half, (k + 1) * half)
                first = ref[at, :]
                step_zero = ordered_ref[at, columns] / theta
                step_one = keep * step_zero + push * first
                solution_ref[at, columns] = step_zero + step_one
                rest_ref[at, columns] = first - RIDGE * step_one - product[:, columns]

        over_tiles(rows, tile)

    return call(
        body, (shape(F32, rows, width), shape(F32, rows, width)),
        (low, high, block, lead, trail, first_lead, first_trail, ordered),
        scratch=[VMEM((rows, width), BF16)],
        flops=2 * rows * rows * width, bytes_=rows * rows * 2 + rows * width * 18,
    )


def final(column, near, block, rest, candidates, bases, coupled, whole_rows=()):
    rows, width = rest.shape
    half = width // 2
    members = lax.axis_size("member")
    count = len(candidates)
    tile_rows = tile_of(rows)
    columns = pl.ds(column * half, half)

    def body(near_ref, block_ref, rest_ref, bases_ref, coupled_ref, *refs):
        others, (out_ref, v, result, sems) = refs[:count], refs[-4:]

        def copy(ref):
            v[...] = ref[...]

        pick(slots(near_ref, members)[1], others, copy)
        copies = []
        for k in range(rows // tile_rows):
            at = pl.ds(k * tile_rows, tile_rows)
            result[at, :] = (rest_ref[at, columns] - dot(block_ref[at, :], v[...])
                             - dot(bases_ref[at, :], coupled_ref[:, columns]))
            copies.append(pltpu.make_async_copy(result.at[at, :], out_ref.at[at, columns], sems.at[k]))
            copies[-1].start()
        for started in copies:
            started.wait()

    args = (near, block, rest, bases, coupled, *candidates, *whole_rows)
    return call(
        body, shape(F32, rows, width), args,
        in_specs=[SMEM_SPEC] + [VMEM_SPEC] * (4 + count) + [ANY_SPEC] * len(whole_rows), out_specs=ANY_SPEC,
        scratch=[VMEM((rows, half), BF16), VMEM((rows, half), F32),
                 pltpu.SemaphoreType.DMA((rows // tile_rows,))],
        flops=2 * rows * rows * half, bytes_=rows * rows * 2 + rows * half * 10,
        aliases={5 + count: 0} if whole_rows else {},
    )


def pair_mate(member):
    return member + 1 - 2 * lax.rem(member, 2)


def gather_messages(message):
    members = lax.axis_size("member")
    rank = message.shape[0]
    if not paired(members):
        others = around(message, "member")
        sources = [functools.partial(lambda k, m: lax.rem(m + (members - k), members), k)
                   for k in range(1, members)]
        return [(other, 0) for other in others], sources
    mates = [(i, i + 1 - 2 * (i % 2)) for i in range(members)]
    mate = lax.ppermute(message, "member", mates)
    pair = pack((message, mate))
    crossed = lax.ppermute(
        pair, "member", [(i, beside_pair(i, members)) for i in range(members)])
    handed = lax.ppermute(crossed, "member", mates)
    return [(mate, 0), (crossed, 0), (crossed, rank), (handed, 0), (handed, rank)], None


def message_views(refs, spots, rank, sources, members):
    member = lax.axis_index("member")
    if sources is not None:
        return [(source(member), ref[row : row + rank, :]) for (ref, row), source in zip(
            zip(refs, [row for _, row in spots]), sources)]
    at_end = (member == 0) | (member == members - 1)
    near_end = jnp.where(member < members // 2, members // 2, members // 2 - 1)
    views = [(pair_mate(member), refs[0][...])]
    for k, number in enumerate((near_end, pair_mate(near_end))):
        rows = slice(k * rank, (k + 1) * rank)
        views.append((number, jnp.where(at_end, refs[3][rows, :], refs[1][rows, :])))
    return views


def merge(own, messages, first_own, first_messages):
    rank = own.shape[0]
    width = first_own.shape[1] - rank
    spots, sources = messages
    first_spots, _ = first_messages
    members = lax.axis_size("member")
    count = len(spots)

    def body(*refs):
        coeffs, firsts, out_ref = refs[:count], refs[count : 2 * count], refs[-1]
        own_ref, first_own_ref = refs[2 * count], refs[2 * count + 1]
        total = dot_tn(first_own_ref[:, width:], own_ref[:, :width])
        for (_, coeff), (_, carried) in zip(
            message_views(coeffs, spots, rank, sources, members),
            message_views(firsts, first_spots, rank, sources, members),
        ):
            total = total + dot_tn(carried[:, width:], coeff[:, :width])
        out_ref[...] = total.astype(BF16)

    args = (*[array for array, _ in spots], *[array for array, _ in first_spots], own, first_own)
    return call(
        body, shape(BF16, rank, width), args,
        flops=2 * rank * rank * width * (count + 1), bytes_=rank * width * 2 * (2 * count + 3),
    )


def pack(blocks):
    rank, width = blocks[0].shape

    def body(*refs):
        for k, ref in enumerate(refs[:-1]):
            refs[-1][k * rank : (k + 1) * rank, :] = ref[...]

    return call(
        body, shape(BF16, rank * len(blocks), width), blocks,
        bytes_=rank * width * 4 * len(blocks),
    )


def inner_of(groups):
    return 2 if groups % 2 == 0 else 1


def all_merged(merged):
    groups = lax.axis_size("group")
    inner = inner_of(groups)
    moved = []
    for k in range(1, groups // inner):
        moved.append(cycle(merged, "group", k * inner))
    if inner == 1:
        return moved, None
    packed = pack((merged, *moved))
    beside = lax.ppermute(packed, "group", [(g, g + 1 - 2 * (g % 2)) for g in range(groups)])
    return moved, beside


def couple(near, couplings, transfer, cross, messages, merged, beside):
    rank = transfer.shape[0]
    width = merged[0].shape[1]
    members = lax.axis_size("member")
    groups = lax.axis_size("group")
    inner = inner_of(groups)
    packed = () if beside is None else (beside,)

    spots, sources = messages
    count = len(spots)

    def body(near_ref, couplings_ref, transfer_ref, cross_ref, *refs):
        coeffs, others, out_ref = refs[:count], refs[count:-1], refs[-1]
        group = lax.axis_index("group")
        crossed = jnp.zeros((rank, width), F32)
        for k in range(1, groups // inner):
            source = lax.rem(group + (groups - k * inner), groups)
            crossed = crossed + dot(cross_ref[source], others[k - 1][...])
        if packed:
            side = group + 1 - 2 * lax.rem(group, 2)
            for k in range(groups // inner):
                source = lax.rem(side + (groups - k * inner), groups)
                crossed = crossed + dot(cross_ref[source], others[-1][k * rank : (k + 1) * rank, :])
        within = dot(transfer_ref[...], crossed.astype(BF16))
        for source, coeff in message_views(coeffs, spots, rank, sources, members):
            far = (source != near_ref[0, 0]) & (source != near_ref[0, 1])
            within = within + jnp.where(far, 1.0, 0.0) * dot(couplings_ref[source], coeff[:, :width])
        out_ref[...] = within.astype(BF16)

    args = (near, couplings, transfer, cross, *[array for array, _ in spots], *merged, *packed)
    return call(
        body, shape(BF16, rank, width), args, scalars=1,
        flops=2 * rank * rank * width * (members + groups), bytes_=rank * width * 2 * (members + groups) * 2,
    )


def around(array, axis):
    moved = []
    for k in range(1, lax.axis_size(axis)):
        moved.append(cycle(array, axis, k))
    return moved


def take_rows(rows, order):
    dims = lax.GatherDimensionNumbers(offset_dims=(1,), collapsed_slice_dims=(0,), start_index_map=(0,))
    return lax.gather(
        rows, order[:, None], dims, (1, rows.shape[1]), unique_indices=True,
        mode=lax.GatherScatterMode.PROMISE_IN_BOUNDS,
    )


def shards(
    points,
    right_sides,
    leaf_order,
    near_leaves,
    bases,
    couplings,
    transfers,
    cross_couplings,
    low_bound,
    high_bound,
):
    transfer = transfers[0]
    couplings = couplings[0]
    cross = cross_couplings[0]
    near = near_leaves
    low, high = low_bound.reshape(1, 1), high_bound.reshape(1, 1)

    points_a, points_b = exchange(points)
    ordered = take_rows(right_sides, leaf_order[0])
    lead, trail, message = prep(ordered, bases, transfer, low, high)
    lead_a, lead_b = exchange(lead)
    messages = gather_messages(message)
    trail_a, trail_b = exchange(trail)
    own_block, rest = self_first(points, ordered, lead, trail, low, high)
    block_a = near_block(0, near, points, points_a)
    block_b = near_block(1, near, points, points_b)
    merged = merge(message, messages, message, messages)
    merged, beside = all_merged(merged)
    rest = subtract_near(near, block_a, rest, lead_a, trail_a)
    coupled = couple(near, couplings, transfer, cross, messages, merged, beside)
    first_lead, lead, coeff = turn(
        0, near, block_b, rest, lead_b, bases, coupled, ordered, low, high)
    first_trail, trail, coeff = turn(
        1, near, block_b, rest, trail_b, bases, coupled, ordered, low, high, (coeff,))

    lead_a, lead_b = exchange(lead)
    coeffs = gather_messages(coeff)
    trail_a, trail_b = exchange(trail)
    solution_rows, rest = self_second(own_block, lead, trail, first_lead, first_trail, ordered, low, high)
    merged = merge(coeff, coeffs, message, messages)
    merged, beside = all_merged(merged)
    rest = subtract_near(near, block_a, rest, lead_a, trail_a)
    coupled = couple(near, couplings, transfer, cross, coeffs, merged, beside)
    residual = final(0, near, block_b, rest, lead_b, bases, coupled)
    residual = final(1, near, block_b, rest, trail_b, bases, coupled, (residual,))
    return solution_rows, residual


def solution(mesh):
    return jax.shard_map(
        shards,
        mesh=mesh,
        in_specs=(
            P(("group", "member"), None),
            P(("group", "member"), None),
            P(("group", "member"), None),
            P(("group", "member"), None),
            P(("group", "member"), None),
            P(("group", "member"), None, None, None),
            P(("group", "member"), None, None),
            P("group", None, None, None),
            P(),
            P(),
        ),
        out_specs=(P(("group", "member"), None), P(("group", "member"), None)),
        check_vma=False,
    )
```

```python
import functools
import math

import jax
import jax.numpy as jnp
from jax import lax
from jax.experimental import pallas as pl
from jax.experimental.pallas import tpu as pltpu
from jax.sharding import PartitionSpec as P


RIDGE = 0.5
KERNEL_WIDTH = 8.0
REACH = 2
F32 = jnp.float32
BF16 = jnp.bfloat16
VMEM = pltpu.VMEM
ANY = pl.ANY


def cycle(array, axis, by):
    count = lax.axis_size(axis)
    return lax.ppermute(array, axis, [(i, (i + by) % count) for i in range(count)])


def tile_of(rows):
    return 512 if rows % 512 == 0 else rows


def over_tiles(rows, body):
    tile = tile_of(rows)

    def step(k, carry):
        body(pl.ds(pl.multiple_of(k * tile, tile), tile))
        return carry

    lax.fori_loop(0, rows // tile, step, 0)


def shape(dtype, *dims):
    return jax.ShapeDtypeStruct(dims, dtype)


SMEM_SPEC = pl.BlockSpec(memory_space=pltpu.SMEM)
ANY_SPEC = pl.BlockSpec(memory_space=ANY)


VMEM_SPEC = pl.BlockSpec(memory_space=VMEM)
HBM_SPEC = pl.BlockSpec(memory_space=pltpu.HBM)


def call(body, out, args, scratch=(), scalars=0, in_specs=None, out_specs=None, flops=0, bytes_=0, exps=0,
         aliases=None):
    many = isinstance(out, tuple)
    return pl.pallas_call(
        body,
        out_shape=out,
        in_specs=in_specs or [SMEM_SPEC] * scalars + [VMEM_SPEC] * (len(args) - scalars),
        out_specs=out_specs or ((VMEM_SPEC,) * len(out) if many else VMEM_SPEC),
        scratch_shapes=list(scratch),
        input_output_aliases=aliases or {},
        cost_estimate=pl.CostEstimate(flops=flops, bytes_accessed=bytes_, transcendentals=exps),
        compiler_params=pltpu.CompilerParams(vmem_limit_bytes=20 * 1024 * 1024),
    )(*args)


def dot(left, right):
    return jnp.dot(left, right, preferred_element_type=F32)


def dot_tn(left, right):
    return lax.dot_general(left, right, (((0,), (0,)), ((), ())), preferred_element_type=F32)


def dot_nt(left, right):
    return lax.dot_general(left, right, (((1,), (1,)), ((), ())), preferred_element_type=F32)


def pieces(value):
    first = value.astype(BF16).astype(F32)
    rest = value - first
    second = rest.astype(BF16).astype(F32)
    return first, second, rest - second


def augmented(block, left):
    rows, dims = block.shape
    wide = block.astype(F32)
    norm = jnp.sum(wide * wide, axis=1, keepdims=True)
    value = -norm / KERNEL_WIDTH
    if left:
        value = value + (dims / 16.0 - math.log(2.0 * rows))
        block = (wide * (2.0 / KERNEL_WIDTH)).astype(BF16)
    lane = lax.broadcasted_iota(jnp.int32, (rows, 128), 1)
    at, ones_at = (0, 3) if left else (3, 0)
    extra = jnp.where((lane >= ones_at) & (lane < ones_at + 3), 1.0, 0.0)
    for k, piece in enumerate(pieces(value)):
        extra = jnp.where(lane == at + k, piece, extra)
    return block, extra.astype(BF16)


def fill_augmented(target, block, left):
    dims = block.shape[1]
    main, extra = augmented(block, left)
    target[:, :dims] = main
    target[:, dims:] = extra


def kernel_tile(left_tile, right_all):
    return jnp.exp(dot_nt(left_tile, right_all)).astype(BF16)


def pick(choice, candidates, use):
    for k, candidate in enumerate(candidates):
        @pl.when(choice == k)
        def _():
            use(candidate)


def paired(members):
    return members == 2 * REACH


def at_end(member, members):
    return (member == 0) | (member == members - 1)


def slots(near_ref, members):
    member = lax.axis_index("member")
    one = near_ref[0, 0] - member
    two = near_ref[0, 1] - member
    if paired(members):
        toward = 1 - 2 * lax.rem(member, 2)
        outer = (one == toward) | (two == toward)
        inner = (one == -toward) | (two == -toward)
        return jnp.where(outer, 0, 1), jnp.where(outer & inner, 0, 1)

    def index(offset):
        return jnp.where(offset == -1, 0, jnp.where(offset == 1, 1, jnp.where(offset == -2, 2, 3)))

    return index(one), index(two)


def with_slot_b(near_ref, members, block_ref, candidates, use):
    choice = slots(near_ref, members)[1]
    for k, ref in enumerate(candidates):
        @pl.when(choice == k)
        def _():
            use(lambda at: dot(block_ref[at, :], ref[...]))


def beside_pair(member, members):
    other = member - 1 if member % 2 == 0 else member + 1
    return other if 0 <= other < members else member


def permute(block, pairs):
    return lax.ppermute(block, "member", pairs)


def mates(members):
    return [(i, i + 1 - 2 * (i % 2)) for i in range(members)]


def hop(block):
    members = lax.axis_size("member")
    inner = permute(block, [(i, beside_pair(i, members)) for i in range(members)])
    return inner, permute(block, mates(members))


def across(inner):
    members = lax.axis_size("member")
    beside = [beside_pair(i, members) for i in range(members)]
    return permute(
        inner, [(i, b + REACH if b + REACH < members else b - REACH) for i, b in enumerate(beside)])


def exchange(block):
    members = lax.axis_size("member")
    up = [(i, i + 1) for i in range(members - 1)]
    down = [(i + 1, i) for i in range(members - 1)]
    before = permute(block, up)
    after = permute(block, down)
    return before, after, permute(before, up), permute(after, down)


def factors(low_ref, high_ref, width):
    low = jnp.broadcast_to(low_ref[...], (1, width))
    high = jnp.broadcast_to(high_ref[...], (1, width))
    theta = (high + low) / 2.0
    delta = (high - low) / 2.0
    sigma = theta / delta
    rho_zero = 1.0 / sigma
    rho_one = 1.0 / (2.0 * sigma - rho_zero)
    return theta, rho_one * rho_zero, 2.0 * rho_one / delta


def start_rows(ordered, low, high):
    rows, width = ordered.shape
    half = width // 2

    def body(low_ref, high_ref, ordered_ref, lead_ref, trail_ref):
        theta, _, _ = factors(low_ref, high_ref, width)

        def tile(at):
            v = (ordered_ref[at, :] / theta).astype(BF16)
            lead_ref[at, :] = v[:, :half]
            trail_ref[at, :] = v[:, half:]

        over_tiles(rows, tile)

    return call(
        body, (shape(BF16, rows, half), shape(BF16, rows, width - half)), (low, high, ordered),
        flops=rows * width, bytes_=rows * width * 6,
    )


def start_message(lead, trail, bases, transfer):
    rows, half = lead.shape
    rank = bases.shape[1]
    width = half + trail.shape[1]

    def body(lead_ref, trail_ref, bases_ref, transfer_ref, message_ref, v):
        join(lead_ref, trail_ref, v)
        message_ref[:, :width] = dot_tn(bases_ref[...], v[...]).astype(BF16)
        message_ref[:, width:] = transfer_ref[...]

    return call(
        body, shape(BF16, rank, width + rank), (lead, trail, bases, transfer),
        scratch=[VMEM((rows, width), BF16)],
        flops=2 * rows * width * rank, bytes_=rows * width * 2 + rows * rank * 2,
    )


def join(lead_ref, trail_ref, target):
    half = trail_ref.shape[1]
    target[:, :half] = lead_ref[...]
    target[:, half:] = trail_ref[...]


def self_first(points, ordered, lead, trail, low, high):
    rows, width = ordered.shape
    dims = points.shape[1]

    def body(low_ref, high_ref, points_ref, ordered_ref, lead_ref, trail_ref, block_ref, rest_ref,
             left, right, v):
        theta, _, _ = factors(low_ref, high_ref, width)
        join(lead_ref, trail_ref, v)
        fill_augmented(left, points_ref[...], True)
        fill_augmented(right, points_ref[...], False)

        def tile(at):
            block = kernel_tile(left[at, :], right[...])
            block_ref[at, :] = block
            own = ordered_ref[at, :]
            rest_ref[at, :] = own - RIDGE * (own / theta) - dot(block, v[...])

        over_tiles(rows, tile)

    return call(
        body, (shape(BF16, rows, rows), shape(F32, rows, width)),
        (low, high, points, ordered, lead, trail),
        scratch=[VMEM((rows, dims + 128), BF16), VMEM((rows, dims + 128), BF16), VMEM((rows, width), BF16)],
        flops=2 * rows * rows * (width + dims), bytes_=rows * rows * 2 + rows * width * 10,
        exps=rows * rows,
    )


def near_block(which, near, points, candidates):
    rows, dims = points.shape
    members = lax.axis_size("member")
    count = len(candidates)

    def body(near_ref, points_ref, *rest):
        others, (block_ref, left, right) = rest[:count], rest[count:]
        fill_augmented(left, points_ref[...], True)
        pick(slots(near_ref, members)[which], others,
             lambda points_of: fill_augmented(right, points_of[...], False))

        def tile(at):
            block_ref[at, :] = kernel_tile(left[at, :], right[...])

        over_tiles(rows, tile)

    return call(
        body, shape(BF16, rows, rows), (near, points, *candidates), scalars=1,
        scratch=[VMEM((rows, dims + 128), BF16), VMEM((rows, dims + 128), BF16)],
        flops=2 * rows * rows * dims, bytes_=rows * rows * 2 + rows * dims * 4, exps=rows * rows,
    )


def subtract_near(near, block, rest, leads, trails):
    rows, width = rest.shape
    members = lax.axis_size("member")
    count = len(leads)

    def body(near_ref, block_ref, rest_ref, *refs):
        pairs = list(zip(refs[:count], refs[count : 2 * count]))
        out_ref, v = refs[2 * count :]
        pick(slots(near_ref, members)[0], pairs, lambda pair: join(*pair, v))

        def tile(at):
            out_ref[at, :] = rest_ref[at, :] - dot(block_ref[at, :], v[...])

        over_tiles(rows, tile)

    return call(
        body, shape(F32, rows, width), (near, block, rest, *leads, *trails), scalars=1,
        scratch=[VMEM((rows, width), BF16)],
        flops=2 * rows * rows * width, bytes_=rows * rows * 2 + rows * width * 10,
    )


def turn(column, near, block, rest, candidates, bases, coupled, ordered, low, high, joined=()):
    rows, width = rest.shape
    rank = bases.shape[1]
    half = width // 2
    members = lax.axis_size("member")
    count = len(candidates)
    kept = len(joined)
    columns = slice(column * half, (column + 1) * half)

    def body(near_ref, low_ref, high_ref, block_ref, rest_ref, bases_ref, coupled_ref, ordered_ref, *refs):
        others, joined_refs = refs[:count], refs[count : count + kept]
        first_ref, v_ref, coeff_ref, total = refs[count + kept :]
        theta, keep, push = factors(low_ref, high_ref, half)
        total[...] = jnp.zeros_like(total)

        def use(slot_b):
            def tile(at):
                own = bases_ref[at, :]
                first = rest_ref[at, columns] - slot_b(at) - dot(own, coupled_ref[:, columns])
                first_ref[at, :] = first
                moved = (keep * (ordered_ref[at, columns] / theta) + push * first).astype(BF16)
                v_ref[at, :] = moved
                total[...] += dot_tn(own, moved)

            over_tiles(rows, tile)

        with_slot_b(near_ref, members, block_ref, others, use)
        for joined_ref in joined_refs:
            coeff_ref[:, :half] = joined_ref[...]
        coeff_ref[:, kept * half :] = total[...].astype(BF16)

    return call(
        body,
        (shape(F32, rows, half), shape(BF16, rows, half), shape(BF16, rank, half * (kept + 1))),
        (near, low, high, block, rest, bases, coupled, ordered, *candidates, *joined), scalars=1,
        scratch=[VMEM((rank, half), F32)],
        flops=2 * rows * rows * half, bytes_=rows * rows * 2 + rows * half * 16,
    )


def self_second(block, lead, trail, first_lead, first_trail, ordered, low, high):
    rows, width = ordered.shape
    half = width // 2

    def body(low_ref, high_ref, block_ref, lead_ref, trail_ref, first_lead_ref, first_trail_ref, ordered_ref,
             solution_ref, rest_ref, v):
        join(lead_ref, trail_ref, v)
        theta, keep, push = factors(low_ref, high_ref, half)

        def tile(at):
            product = dot(block_ref[at, :], v[...])
            for k, ref in enumerate((first_lead_ref, first_trail_ref)):
                columns = slice(k * half, (k + 1) * half)
                first = ref[at, :]
                step_zero = ordered_ref[at, columns] / theta
                step_one = keep * step_zero + push * first
                solution_ref[at, columns] = step_zero + step_one
                rest_ref[at, columns] = first - RIDGE * step_one - product[:, columns]

        over_tiles(rows, tile)

    return call(
        body, (shape(F32, rows, width), shape(F32, rows, width)),
        (low, high, block, lead, trail, first_lead, first_trail, ordered),
        scratch=[VMEM((rows, width), BF16)],
        flops=2 * rows * rows * width, bytes_=rows * rows * 2 + rows * width * 18,
    )


def final(column, near, block, rest, candidates, bases, coupled, written=()):
    rows, width = rest.shape
    half = width // 2
    members = lax.axis_size("member")
    count = len(candidates)
    tile_rows = tile_of(rows)
    columns = pl.ds(column * half, half)

    def body(near_ref, block_ref, rest_ref, bases_ref, coupled_ref, *refs):
        others, (out_ref, result, sems) = refs[:count], refs[-3:]

        def use(slot_b):
            copies = []
            for k in range(rows // tile_rows):
                at = pl.ds(k * tile_rows, tile_rows)
                result[at, :] = (
                    rest_ref[at, columns] - slot_b(at) - dot(bases_ref[at, :], coupled_ref[:, columns]))
                copies.append(pltpu.make_async_copy(result.at[at, :], out_ref.at[at, columns], sems.at[k]))
                copies[-1].start()
            for started in copies:
                started.wait()

        with_slot_b(near_ref, members, block_ref, others, use)

    return call(
        body, shape(F32, rows, width), (near, block, rest, bases, coupled, *candidates, *written),
        in_specs=[SMEM_SPEC] + [VMEM_SPEC] * (4 + count) + [ANY_SPEC] * len(written), out_specs=ANY_SPEC,
        scratch=[VMEM((rows, half), F32), pltpu.SemaphoreType.DMA((rows // tile_rows,))],
        flops=2 * rows * rows * half, bytes_=rows * rows * 2 + rows * half * 10,
        aliases={5 + count: 0} if written else {},
    )


def pair_mate(member):
    return member + 1 - 2 * lax.rem(member, 2)


def gather_messages(message):
    members = lax.axis_size("member")
    rank = message.shape[0]
    if not paired(members):
        others = around(message, "member")
        sources = [functools.partial(lambda k, m: lax.rem(m + (members - k), members), k)
                   for k in range(1, members)]
        return [(other, 0) for other in others], sources
    mate = permute(message, mates(members))
    pair = pack((message, mate))
    crossed = permute(pair, [(i, beside_pair(i, members)) for i in range(members)])
    handed = permute(crossed, mates(members))
    return [(mate, 0), (crossed, 0), (crossed, rank), (handed, 0), (handed, rank)], None


def message_views(refs, spots, rank, sources, members):
    member = lax.axis_index("member")
    if sources is not None:
        return [(source(member), ref[row : row + rank, :]) for (ref, row), source in zip(
            zip(refs, [row for _, row in spots]), sources)]
    end = at_end(member, members)
    near_end = jnp.where(member < members // 2, members // 2, members // 2 - 1)
    views = [(pair_mate(member), refs[0][...])]
    for k, number in enumerate((near_end, pair_mate(near_end))):
        rows = slice(k * rank, (k + 1) * rank)
        views.append((number, jnp.where(end, refs[3][rows, :], refs[1][rows, :])))
    return views


def merge(own, messages, first_own, first_messages):
    rank = own.shape[0]
    width = first_own.shape[1] - rank
    spots, sources = messages
    first_spots, _ = first_messages
    members = lax.axis_size("member")
    count = len(spots)

    def body(*refs):
        coeffs, firsts, out_ref = refs[:count], refs[count : 2 * count], refs[-1]
        own_ref, first_own_ref = refs[2 * count], refs[2 * count + 1]
        total = dot_tn(first_own_ref[:, width:], own_ref[:, :width])
        for (_, coeff), (_, carried) in zip(
            message_views(coeffs, spots, rank, sources, members),
            message_views(firsts, first_spots, rank, sources, members),
        ):
            total = total + dot_tn(carried[:, width:], coeff[:, :width])
        out_ref[...] = total.astype(BF16)

    args = (*[array for array, _ in spots], *[array for array, _ in first_spots], own, first_own)
    return call(
        body, shape(BF16, rank, width), args,
        flops=2 * rank * rank * width * (count + 1), bytes_=rank * width * 2 * (2 * count + 3),
    )


def pack(blocks):
    rank, width = blocks[0].shape

    def body(*refs):
        for k, ref in enumerate(refs[:-1]):
            refs[-1][k * rank : (k + 1) * rank, :] = ref[...]

    return call(
        body, shape(BF16, rank * len(blocks), width), blocks,
        bytes_=rank * width * 4 * len(blocks),
    )


def inner_of(groups):
    return 2 if groups % 2 == 0 else 1


def all_merged(merged):
    groups = lax.axis_size("group")
    inner = inner_of(groups)
    moved = []
    for k in range(1, groups // inner):
        moved.append(cycle(merged, "group", k * inner))
    if inner == 1:
        return moved, None
    packed = pack((merged, *moved))
    beside = lax.ppermute(packed, "group", [(g, g + 1 - 2 * (g % 2)) for g in range(groups)])
    return moved, beside


def couple(near, couplings, transfer, cross, messages, merged, beside):
    rank = transfer.shape[0]
    width = merged[0].shape[1]
    members = lax.axis_size("member")
    groups = lax.axis_size("group")
    inner = inner_of(groups)
    packed = () if beside is None else (beside,)

    spots, sources = messages
    count = len(spots)

    def body(near_ref, couplings_ref, transfer_ref, cross_ref, *refs):
        coeffs, others, out_ref = refs[:count], refs[count:-1], refs[-1]
        group = lax.axis_index("group")
        crossed = jnp.zeros((rank, width), F32)
        for k in range(1, groups // inner):
            source = lax.rem(group + (groups - k * inner), groups)
            crossed = crossed + dot(cross_ref[source], others[k - 1][...])
        if packed:
            side = group + 1 - 2 * lax.rem(group, 2)
            for k in range(groups // inner):
                source = lax.rem(side + (groups - k * inner), groups)
                crossed = crossed + dot(cross_ref[source], others[-1][k * rank : (k + 1) * rank, :])
        within = dot(transfer_ref[...], crossed.astype(BF16))
        for source, coeff in message_views(coeffs, spots, rank, sources, members):
            far = (source != near_ref[0, 0]) & (source != near_ref[0, 1])
            within = within + jnp.where(far, 1.0, 0.0) * dot(couplings_ref[source], coeff[:, :width])
        out_ref[...] = within.astype(BF16)

    args = (near, couplings, transfer, cross, *[array for array, _ in spots], *merged, *packed)
    return call(
        body, shape(BF16, rank, width), args, scalars=1,
        flops=2 * rank * rank * width * (members + groups), bytes_=rank * width * 2 * (members + groups) * 2,
    )


def around(array, axis):
    moved = []
    for k in range(1, lax.axis_size(axis)):
        moved.append(cycle(array, axis, k))
    return moved


def take_rows(rows, order):
    dims = lax.GatherDimensionNumbers(offset_dims=(1,), collapsed_slice_dims=(0,), start_index_map=(0,))
    return lax.gather(
        rows, order[:, None], dims, (1, rows.shape[1]), unique_indices=True,
        mode=lax.GatherScatterMode.PROMISE_IN_BOUNDS,
    )


def shards(
    points,
    right_sides,
    leaf_order,
    near_leaves,
    bases,
    couplings,
    transfers,
    cross_couplings,
    low_bound,
    high_bound,
):
    transfer = transfers[0]
    couplings = couplings[0]
    cross = cross_couplings[0]
    near = near_leaves
    low, high = low_bound.reshape(1, 1), high_bound.reshape(1, 1)

    line = paired(lax.axis_size("member"))

    def moved(block):
        if not line:
            blocks = exchange(block)
            return blocks, blocks
        inner, outer = hop(block)
        return (outer, inner), (inner, across(inner))

    points_a, points_b = moved(points)
    block_a = near_block(0, near, points, points_a)
    block_b = near_block(1, near, points, points_b)
    ordered = take_rows(right_sides, leaf_order[0])
    lead, trail = start_rows(ordered, low, high)
    message = start_message(lead, trail, bases, transfer)
    messages = gather_messages(message)
    lead_a, lead_b = moved(lead)
    trail_a, trail_b = moved(trail)
    own_block, rest = self_first(points, ordered, lead, trail, low, high)
    merged = merge(message, messages, message, messages)
    merged, beside = all_merged(merged)
    rest = subtract_near(near, block_a, rest, lead_a, trail_a)
    coupled = couple(near, couplings, transfer, cross, messages, merged, beside)
    first_lead, lead, coeff = turn(0, near, block_b, rest, lead_b, bases, coupled, ordered, low, high)
    first_trail, trail, coeff = turn(
        1, near, block_b, rest, trail_b, bases, coupled, ordered, low, high, (coeff,))

    coeffs = gather_messages(coeff)
    lead_a, lead_b = moved(lead)
    trail_a, trail_b = moved(trail)
    solution_rows, rest = self_second(own_block, lead, trail, first_lead, first_trail, ordered, low, high)
    merged = merge(coeff, coeffs, message, messages)
    merged, beside = all_merged(merged)
    rest = subtract_near(near, block_a, rest, lead_a, trail_a)
    coupled = couple(near, couplings, transfer, cross, coeffs, merged, beside)
    residual = final(0, near, block_b, rest, lead_b, bases, coupled)
    residual = final(1, near, block_b, rest, trail_b, bases, coupled, (residual,))
    return solution_rows, residual


def solution(mesh):
    return jax.shard_map(
        shards,
        mesh=mesh,
        in_specs=(
            P(("group", "member"), None),
            P(("group", "member"), None),
            P(("group", "member"), None),
            P(("group", "member"), None),
            P(("group", "member"), None),
            P(("group", "member"), None, None, None),
            P(("group", "member"), None, None),
            P("group", None, None, None),
            P(),
            P(),
        ),
        out_specs=(P(("group", "member"), None), P(("group", "member"), None)),
        check_vma=False,
    )
```

```python
import math

import jax
import jax.numpy as jnp
from jax import lax
from jax.experimental import pallas as pl
from jax.experimental.pallas import tpu as pltpu
from jax.sharding import PartitionSpec as P


RIDGE = 0.5
KERNEL_WIDTH = 8.0
REACH = 2
F32 = jnp.float32
BF16 = jnp.bfloat16
VMEM = pltpu.VMEM
ANY = pl.ANY


def cycle(array, axis, by):
    count = lax.axis_size(axis)
    return lax.ppermute(array, axis, [(i, (i + by) % count) for i in range(count)])


def tile_of(rows):
    return 512 if rows % 512 == 0 else rows


def over_tiles(rows, body):
    tile = tile_of(rows)

    def step(k, carry):
        body(pl.ds(pl.multiple_of(k * tile, tile), tile))
        return carry

    lax.fori_loop(0, rows // tile, step, 0)


def shape(dtype, *dims):
    return jax.ShapeDtypeStruct(dims, dtype)


SMEM_SPEC = pl.BlockSpec(memory_space=pltpu.SMEM)
ANY_SPEC = pl.BlockSpec(memory_space=ANY)


VMEM_SPEC = pl.BlockSpec(memory_space=VMEM)
HBM_SPEC = pl.BlockSpec(memory_space=pltpu.HBM)


def call(body, out, args, scratch=(), scalars=0, in_specs=None, out_specs=None, flops=0, bytes_=0, exps=0,
         aliases=None):
    many = isinstance(out, tuple)
    return pl.pallas_call(
        body,
        out_shape=out,
        in_specs=in_specs or [SMEM_SPEC] * scalars + [VMEM_SPEC] * (len(args) - scalars),
        out_specs=out_specs or ((VMEM_SPEC,) * len(out) if many else VMEM_SPEC),
        scratch_shapes=list(scratch),
        input_output_aliases=aliases or {},
        cost_estimate=pl.CostEstimate(flops=flops, bytes_accessed=bytes_, transcendentals=exps),
        compiler_params=pltpu.CompilerParams(vmem_limit_bytes=20 * 1024 * 1024),
    )(*args)


def dot(left, right):
    return jnp.dot(left, right, preferred_element_type=F32)


def dot_tn(left, right):
    return lax.dot_general(left, right, (((0,), (0,)), ((), ())), preferred_element_type=F32)


def dot_nt(left, right):
    return lax.dot_general(left, right, (((1,), (1,)), ((), ())), preferred_element_type=F32)


def pieces(value):
    first = value.astype(BF16).astype(F32)
    rest = value - first
    second = rest.astype(BF16).astype(F32)
    return first, second, rest - second


def augmented(block, left):
    rows, dims = block.shape
    wide = block.astype(F32)
    norm = jnp.sum(wide * wide, axis=1, keepdims=True)
    value = -norm / KERNEL_WIDTH
    if left:
        value = value + (dims / 16.0 - math.log(2.0 * rows))
        block = (wide * (2.0 / KERNEL_WIDTH)).astype(BF16)
    lane = lax.broadcasted_iota(jnp.int32, (rows, 128), 1)
    at, ones_at = (0, 3) if left else (3, 0)
    extra = jnp.where((lane >= ones_at) & (lane < ones_at + 3), 1.0, 0.0)
    for k, piece in enumerate(pieces(value)):
        extra = jnp.where(lane == at + k, piece, extra)
    return block, extra.astype(BF16)


def fill_augmented(target, block, left):
    dims = block.shape[1]
    main, extra = augmented(block, left)
    target[:, :dims] = main
    target[:, dims:] = extra


def kernel_tile(left_tile, right_all):
    return jnp.exp(dot_nt(left_tile, right_all)).astype(BF16)


def pick(choice, candidates, use):
    for k, candidate in enumerate(candidates):
        @pl.when(choice == k)
        def _():
            use(candidate)


def paired(members):
    return members == 2 * REACH


def at_end(member, members):
    return (member == 0) | (member == members - 1)


def slots(near_ref, members):
    member = lax.axis_index("member")
    one = near_ref[0, 0] - member
    two = near_ref[0, 1] - member
    if paired(members):
        toward = 1 - 2 * lax.rem(member, 2)
        outer = (one == toward) | (two == toward)
        inner = (one == -toward) | (two == -toward)
        return jnp.where(outer, 0, 1), jnp.where(outer & inner, 0, 1)

    def index(offset):
        return jnp.where(offset == -1, 0, jnp.where(offset == 1, 1, jnp.where(offset == -2, 2, 3)))

    return index(one), index(two)


def with_slot_b(near_ref, members, block_ref, candidates, use):
    choice = slots(near_ref, members)[1]
    for k, ref in enumerate(candidates):
        @pl.when(choice == k)
        def _():
            use(lambda at: dot(block_ref[at, :], ref[...]))


def beside_pair(member, members):
    other = member - 1 if member % 2 == 0 else member + 1
    return other if 0 <= other < members else member


def permute(block, pairs):
    return lax.ppermute(block, "member", pairs)


def mates(members):
    return [(i, i + 1 - 2 * (i % 2)) for i in range(members)]


def hop(block):
    members = lax.axis_size("member")
    inner = permute(block, [(i, beside_pair(i, members)) for i in range(members)])
    return inner, permute(block, mates(members))


def across(inner):
    members = lax.axis_size("member")
    beside = [beside_pair(i, members) for i in range(members)]
    return permute(
        inner, [(i, b + REACH if b + REACH < members else b - REACH) for i, b in enumerate(beside)])


def exchange(block):
    members = lax.axis_size("member")
    up = [(i, i + 1) for i in range(members - 1)]
    down = [(i + 1, i) for i in range(members - 1)]
    before = permute(block, up)
    after = permute(block, down)
    return before, after, permute(before, up), permute(after, down)


def factors(low_ref, high_ref, width):
    low = jnp.broadcast_to(low_ref[...], (1, width))
    high = jnp.broadcast_to(high_ref[...], (1, width))
    theta = (high + low) / 2.0
    delta = (high - low) / 2.0
    sigma = theta / delta
    rho_zero = 1.0 / sigma
    rho_one = 1.0 / (2.0 * sigma - rho_zero)
    return theta, rho_one * rho_zero, 2.0 * rho_one / delta


def start_rows(ordered, low, high):
    rows, width = ordered.shape
    half = width // 2

    def body(low_ref, high_ref, ordered_ref, lead_ref, trail_ref):
        theta, _, _ = factors(low_ref, high_ref, width)

        def tile(at):
            v = (ordered_ref[at, :] / theta).astype(BF16)
            lead_ref[at, :] = v[:, :half]
            trail_ref[at, :] = v[:, half:]

        over_tiles(rows, tile)

    return call(
        body, (shape(BF16, rows, half), shape(BF16, rows, width - half)), (low, high, ordered),
        flops=rows * width, bytes_=rows * width * 6,
    )


def start_message(lead, trail, bases, transfer):
    rows, half = lead.shape
    rank = bases.shape[1]
    width = half + trail.shape[1]

    def body(lead_ref, trail_ref, bases_ref, transfer_ref, message_ref, v):
        join(lead_ref, trail_ref, v)
        message_ref[:, :width] = dot_tn(bases_ref[...], v[...]).astype(BF16)
        message_ref[:, width:] = transfer_ref[...]

    return call(
        body, shape(BF16, rank, width + rank), (lead, trail, bases, transfer),
        scratch=[VMEM((rows, width), BF16)],
        flops=2 * rows * width * rank, bytes_=rows * width * 2 + rows * rank * 2,
    )


def join(lead_ref, trail_ref, target):
    half = trail_ref.shape[1]
    target[:, :half] = lead_ref[...]
    target[:, half:] = trail_ref[...]


def self_first(points, ordered, lead, trail, low, high):
    rows, width = ordered.shape
    dims = points.shape[1]

    def body(low_ref, high_ref, points_ref, ordered_ref, lead_ref, trail_ref, block_ref, rest_ref,
             left, right, v):
        theta, _, _ = factors(low_ref, high_ref, width)
        join(lead_ref, trail_ref, v)
        fill_augmented(left, points_ref[...], True)
        fill_augmented(right, points_ref[...], False)

        def tile(at):
            block = kernel_tile(left[at, :], right[...])
            block_ref[at, :] = block
            own = ordered_ref[at, :]
            rest_ref[at, :] = own - RIDGE * (own / theta) - dot(block, v[...])

        over_tiles(rows, tile)

    return call(
        body, (shape(BF16, rows, rows), shape(F32, rows, width)),
        (low, high, points, ordered, lead, trail),
        scratch=[VMEM((rows, dims + 128), BF16), VMEM((rows, dims + 128), BF16), VMEM((rows, width), BF16)],
        flops=2 * rows * rows * (width + dims), bytes_=rows * rows * 2 + rows * width * 10,
        exps=rows * rows,
    )


def near_block(which, near, points, candidates):
    rows, dims = points.shape
    members = lax.axis_size("member")
    count = len(candidates)

    def body(near_ref, points_ref, *rest):
        others, (block_ref, left, right) = rest[:count], rest[count:]
        fill_augmented(left, points_ref[...], True)
        pick(slots(near_ref, members)[which], others,
             lambda points_of: fill_augmented(right, points_of[...], False))

        def tile(at):
            block_ref[at, :] = kernel_tile(left[at, :], right[...])

        over_tiles(rows, tile)

    return call(
        body, shape(BF16, rows, rows), (near, points, *candidates), scalars=1,
        scratch=[VMEM((rows, dims + 128), BF16), VMEM((rows, dims + 128), BF16)],
        flops=2 * rows * rows * dims, bytes_=rows * rows * 2 + rows * dims * 4, exps=rows * rows,
    )


def subtract_near(near, block, rest, leads, trails):
    rows, width = rest.shape
    members = lax.axis_size("member")
    count = len(leads)

    def body(near_ref, block_ref, rest_ref, *refs):
        pairs = list(zip(refs[:count], refs[count : 2 * count]))
        out_ref, v = refs[2 * count :]
        pick(slots(near_ref, members)[0], pairs, lambda pair: join(*pair, v))

        def tile(at):
            out_ref[at, :] = rest_ref[at, :] - dot(block_ref[at, :], v[...])

        over_tiles(rows, tile)

    return call(
        body, shape(F32, rows, width), (near, block, rest, *leads, *trails), scalars=1,
        scratch=[VMEM((rows, width), BF16)],
        flops=2 * rows * rows * width, bytes_=rows * rows * 2 + rows * width * 10,
    )


def turn(column, near, block, rest, candidates, bases, coupled, ordered, low, high, joined=()):
    rows, width = rest.shape
    rank = bases.shape[1]
    half = width // 2
    members = lax.axis_size("member")
    count = len(candidates)
    kept = len(joined)
    columns = slice(column * half, (column + 1) * half)

    def body(near_ref, low_ref, high_ref, block_ref, rest_ref, bases_ref, coupled_ref, ordered_ref, *refs):
        others, joined_refs = refs[:count], refs[count : count + kept]
        first_ref, v_ref, coeff_ref, total = refs[count + kept :]
        theta, keep, push = factors(low_ref, high_ref, half)
        total[...] = jnp.zeros_like(total)

        def use(slot_b):
            def tile(at):
                own = bases_ref[at, :]
                first = rest_ref[at, columns] - slot_b(at) - dot(own, coupled_ref[:, columns])
                first_ref[at, :] = first
                moved = (keep * (ordered_ref[at, columns] / theta) + push * first).astype(BF16)
                v_ref[at, :] = moved
                total[...] += dot_tn(own, moved)

            over_tiles(rows, tile)

        with_slot_b(near_ref, members, block_ref, others, use)
        for joined_ref in joined_refs:
            coeff_ref[:, :half] = joined_ref[...]
        coeff_ref[:, kept * half :] = total[...].astype(BF16)

    return call(
        body,
        (shape(F32, rows, half), shape(BF16, rows, half), shape(BF16, rank, half * (kept + 1))),
        (near, low, high, block, rest, bases, coupled, ordered, *candidates, *joined), scalars=1,
        scratch=[VMEM((rank, half), F32)],
        flops=2 * rows * rows * half, bytes_=rows * rows * 2 + rows * half * 16,
    )


def self_second(block, lead, trail, first_lead, first_trail, ordered, low, high):
    rows, width = ordered.shape
    half = width // 2

    def body(low_ref, high_ref, block_ref, lead_ref, trail_ref, first_lead_ref, first_trail_ref, ordered_ref,
             solution_ref, rest_ref, v):
        join(lead_ref, trail_ref, v)
        theta, keep, push = factors(low_ref, high_ref, half)

        def tile(at):
            product = dot(block_ref[at, :], v[...])
            for k, ref in enumerate((first_lead_ref, first_trail_ref)):
                columns = slice(k * half, (k + 1) * half)
                first = ref[at, :]
                step_zero = ordered_ref[at, columns] / theta
                step_one = keep * step_zero + push * first
                solution_ref[at, columns] = step_zero + step_one
                rest_ref[at, columns] = first - RIDGE * step_one - product[:, columns]

        over_tiles(rows, tile)

    return call(
        body, (shape(F32, rows, width), shape(F32, rows, width)),
        (low, high, block, lead, trail, first_lead, first_trail, ordered),
        scratch=[VMEM((rows, width), BF16)],
        flops=2 * rows * rows * width, bytes_=rows * rows * 2 + rows * width * 18,
    )


def write_tiles(steps, tile, result, out_ref, columns, sems):
    copies = []
    for k, (first, count) in enumerate(steps):
        at = pl.ds(first, count)
        result[at, :] = tile(at)
        copies.append(pltpu.make_async_copy(result.at[at, :], out_ref.at[at, columns], sems.at[k]))
        copies[-1].start()
    for started in copies:
        started.wait()


def final_lead(near, block, rest, candidates, bases, coupled):
    rows, width = rest.shape
    half = width // 2
    members = lax.axis_size("member")
    count = len(candidates)
    tile_rows = tile_of(rows)
    steps = [(k, tile_rows) for k in range(0, rows, tile_rows)]

    def body(near_ref, block_ref, rest_ref, bases_ref, coupled_ref, *refs):
        others, (out_ref, trail_ref, result, sems) = refs[:count], refs[count:]

        def use(slot_b):
            def tile(at):
                other = rest_ref[at, :] - dot(bases_ref[at, :], coupled_ref[...])
                trail_ref[at, :] = other[:, half:]
                return other[:, :half] - slot_b(at)

            write_tiles(steps, tile, result, out_ref, pl.ds(0, half), sems)

        with_slot_b(near_ref, members, block_ref, others, use)

    return call(
        body, (shape(F32, rows, width), shape(F32, rows, half)),
        (near, block, rest, bases, coupled, *candidates), scalars=1, out_specs=(ANY_SPEC, VMEM_SPEC),
        scratch=[VMEM((rows, half), F32), pltpu.SemaphoreType.DMA((len(steps),))],
        flops=2 * rows * rows * half, bytes_=rows * rows * 2 + rows * half * 10,
    )


def trail_part(near, block, trail, inner, piece):
    rows, half = trail.shape
    members = lax.axis_size("member")
    cut = piece.shape[0]

    def body(near_ref, block_ref, trail_ref, inner_ref, piece_ref, out_ref):
        choice = slots(near_ref, members)[1]

        @pl.when(choice == 0)
        def _():
            def tile(at):
                out_ref[at, :] = trail_ref[at, :] - dot(block_ref[at, :], inner_ref[...])

            over_tiles(rows, tile)

        @pl.when(choice != 0)
        def _():
            def tile(at):
                out_ref[at, :] = trail_ref[at, :] - dot(block_ref[at, :cut], piece_ref[...])

            over_tiles(rows, tile)

    return call(
        body, shape(F32, rows, half), (near, block, trail, inner, piece), scalars=1,
        flops=2 * rows * cut * half, bytes_=rows * cut * 2 + rows * half * 8,
    )


def final_trail(near, block, trail, candidates, first, written):
    rows, half = trail.shape
    members = lax.axis_size("member")
    count = len(candidates)
    tile_rows = tile_of(rows)
    steps = [(k, tile_rows) for k in range(0, rows, tile_rows)]

    def body(near_ref, block_ref, trail_ref, *refs):
        others, (out_ref, result, sems) = refs[:count], refs[-3:]

        def use(slot_b):
            def tile(at):
                return trail_ref[at, :] - slot_b(at)

            write_tiles(steps, tile, result, out_ref, pl.ds(half, half), sems)

        if first is None:
            with_slot_b(near_ref, members, block_ref, others, use)
        else:
            late = slots(near_ref, members)[1] != 0
            pl.when(late)(lambda: use(lambda at: dot(block_ref[at, first:], others[0][...])))
            pl.when(jnp.logical_not(late))(lambda: use(lambda at: 0.0))

    return call(
        body, shape(F32, *written.shape), (near, block, trail, *candidates, written),
        in_specs=[SMEM_SPEC] + [VMEM_SPEC] * (2 + count) + [ANY_SPEC], out_specs=ANY_SPEC,
        scratch=[VMEM((rows, half), F32), pltpu.SemaphoreType.DMA((len(steps),))],
        flops=2 * rows * rows * half, bytes_=rows * rows * 2 + rows * half * 10,
        aliases={3 + count: 0},
    )


def merge_all(message, first, rank):
    members = lax.axis_size("member")
    width = first["own"].shape[1] - rank if first else message.shape[1] - rank
    if not paired(members):
        others = around(message, "member")
        state = {"own": message, "others": others}
        first = first or state
        merged = merge_ring(state, first, rank, width)
        return state, merged
    down = mates(members)
    up = mates(members)
    mate = permute(message, down)
    pair = pack((message, mate))
    crossed = permute(pair, [(i, beside_pair(i, members)) for i in range(members)])
    state = {"own": message, "pair": pair, "crossed": crossed}
    first = first or state
    summed = merge_line(state, first, rank, width)
    handed = permute(summed, up)
    state["handed"] = handed
    return state, choose(summed, handed, width)


def merge_ring(state, first, rank, width):
    count = len(state["others"]) + 1

    def body(*refs):
        total = jnp.zeros((rank, width), F32)
        for coeff, carried in zip(refs[:count], refs[count:-1]):
            total = total + dot_tn(carried[:, width:], coeff[:, :width])
        refs[-1][...] = total.astype(BF16)

    args = (state["own"], *state["others"], first["own"], *first["others"])
    return call(
        body, shape(BF16, rank, width), args,
        flops=2 * rank * rank * width * count, bytes_=rank * width * 4 * count,
    )


def merge_line(state, first, rank, width):
    def body(pair_ref, crossed_ref, first_pair_ref, first_crossed_ref, out_ref):
        total = jnp.zeros((rank, width), F32)
        for coeffs, carried in ((pair_ref, first_pair_ref), (crossed_ref, first_crossed_ref)):
            for rows in (slice(0, rank), slice(rank, 2 * rank)):
                total = total + dot_tn(carried[rows, width:], coeffs[rows, :width])
        out_ref[:, :width] = total.astype(BF16)
        out_ref[:, width:] = crossed_ref[rank:, :width]

    return call(
        body, shape(BF16, rank, 2 * width),
        (state["pair"], state["crossed"], first["pair"], first["crossed"]),
        flops=8 * rank * rank * width, bytes_=rank * width * 16,
    )


def choose(summed, handed, width):
    members = lax.axis_size("member")

    def body(summed_ref, handed_ref, out_ref):
        end = at_end(lax.axis_index("member"), members)
        out_ref[...] = jnp.where(end, handed_ref[:, :width], summed_ref[:, :width])

    return call(
        body, shape(BF16, summed.shape[0], width), (summed, handed),
        bytes_=summed.shape[0] * width * 6,
    )


def coupled_arrays(state):
    if "others" in state:
        return tuple(state["others"])
    return state["pair"], state["crossed"], state["handed"]


def coupled_views(refs, rank, width):
    members = lax.axis_size("member")
    member = lax.axis_index("member")
    if not paired(members):
        return [(lax.rem(member + (members - 1 - k), members), ref[:, :width]) for k, ref in enumerate(refs)]
    pair_ref, crossed_ref, handed_ref = refs
    lower = member < members // 2
    far_end = jnp.where(lower, members - 1, 0)
    far_middle = jnp.where(lower, members // 2, members // 2 - 1)
    own_end = members - 1 - far_end
    end = at_end(member, members)
    from_far_end = jnp.where(end, handed_ref[:, width:], crossed_ref[rank:, :width])
    return [
        (jnp.where(end, far_middle, own_end), pair_ref[rank:, :width]),
        (far_middle, crossed_ref[:rank, :width]),
        (far_end, from_far_end),
    ]


def pack(blocks):
    rank, width = blocks[0].shape

    def body(*refs):
        for k, ref in enumerate(refs[:-1]):
            refs[-1][k * rank : (k + 1) * rank, :] = ref[...]

    return call(
        body, shape(BF16, rank * len(blocks), width), blocks,
        bytes_=rank * width * 4 * len(blocks),
    )


def inner_of(groups):
    return 2 if groups % 2 == 0 else 1


def all_merged(merged):
    groups = lax.axis_size("group")
    inner = inner_of(groups)
    moved = []
    for k in range(1, groups // inner):
        moved.append(cycle(merged, "group", k * inner))
    if inner == 1:
        return moved, None
    packed = pack((merged, *moved))
    beside = lax.ppermute(packed, "group", [(g, g + 1 - 2 * (g % 2)) for g in range(groups)])
    return moved, beside


def couple(near, couplings, transfer, cross, messages, merged, beside):
    rank = transfer.shape[0]
    width = merged[0].shape[1]
    members = lax.axis_size("member")
    groups = lax.axis_size("group")
    inner = inner_of(groups)
    packed = () if beside is None else (beside,)

    arrays = coupled_arrays(messages)
    count = len(arrays)

    def body(near_ref, couplings_ref, transfer_ref, cross_ref, *refs):
        coeffs, others, out_ref = refs[:count], refs[count:-1], refs[-1]
        group = lax.axis_index("group")
        crossed = jnp.zeros((rank, width), F32)
        for k in range(1, groups // inner):
            source = lax.rem(group + (groups - k * inner), groups)
            crossed = crossed + dot(cross_ref[source], others[k - 1][...])
        if packed:
            side = group + 1 - 2 * lax.rem(group, 2)
            for k in range(groups // inner):
                source = lax.rem(side + (groups - k * inner), groups)
                crossed = crossed + dot(cross_ref[source], others[-1][k * rank : (k + 1) * rank, :])
        within = dot(transfer_ref[...], crossed.astype(BF16))
        for source, coeff in coupled_views(coeffs, rank, width):
            far = (source != near_ref[0, 0]) & (source != near_ref[0, 1])
            within = within + jnp.where(far, 1.0, 0.0) * dot(couplings_ref[source], coeff)
        out_ref[...] = within.astype(BF16)

    args = (near, couplings, transfer, cross, *arrays, *merged, *packed)
    return call(
        body, shape(BF16, rank, width), args, scalars=1,
        flops=2 * rank * rank * width * (members + groups), bytes_=rank * width * 2 * (members + groups) * 2,
    )


def around(array, axis):
    moved = []
    for k in range(1, lax.axis_size(axis)):
        moved.append(cycle(array, axis, k))
    return moved


def take_rows(rows, order):
    dims = lax.GatherDimensionNumbers(offset_dims=(1,), collapsed_slice_dims=(0,), start_index_map=(0,))
    return lax.gather(
        rows, order[:, None], dims, (1, rows.shape[1]), unique_indices=True,
        mode=lax.GatherScatterMode.PROMISE_IN_BOUNDS,
    )


def shards(
    points,
    right_sides,
    leaf_order,
    near_leaves,
    bases,
    couplings,
    transfers,
    cross_couplings,
    low_bound,
    high_bound,
):
    transfer = transfers[0]
    couplings = couplings[0]
    cross = cross_couplings[0]
    near = near_leaves
    low, high = low_bound.reshape(1, 1), high_bound.reshape(1, 1)

    line = paired(lax.axis_size("member"))

    def moved(block):
        if not line:
            blocks = exchange(block)
            return blocks, blocks
        inner, outer = hop(block)
        return (outer, inner), (inner, across(inner))

    points_a, points_b = moved(points)
    block_a = near_block(0, near, points, points_a)
    block_b = near_block(1, near, points, points_b)
    ordered = take_rows(right_sides, leaf_order[0])
    lead, trail = start_rows(ordered, low, high)
    message = start_message(lead, trail, bases, transfer)
    rank = transfer.shape[0]
    messages, merged = merge_all(message, None, rank)
    lead_a, lead_b = moved(lead)
    trail_a, trail_b = moved(trail)
    own_block, rest = self_first(points, ordered, lead, trail, low, high)
    merged, beside = all_merged(merged)
    rest = subtract_near(near, block_a, rest, lead_a, trail_a)
    coupled = couple(near, couplings, transfer, cross, messages, merged, beside)
    first_lead, lead, coeff = turn(0, near, block_b, rest, lead_b, bases, coupled, ordered, low, high)
    first_trail, trail, coeff = turn(
        1, near, block_b, rest, trail_b, bases, coupled, ordered, low, high, (coeff,))

    coeffs, merged = merge_all(coeff, messages, rank)
    lead_a, lead_b = moved(lead)
    if line:
        inner, outer = hop(trail)
        trail_a = (outer, inner)
        cut = 2 * trail.shape[0] // 3 if trail.shape[0] % 384 == 0 else trail.shape[0] // 2
        early = across(inner[:cut])
        late = across(inner[cut:])
    else:
        trail_a, trail_b = moved(trail)
    solution_rows, rest = self_second(own_block, lead, trail, first_lead, first_trail, ordered, low, high)
    merged, beside = all_merged(merged)
    rest = subtract_near(near, block_a, rest, lead_a, trail_a)
    coupled = couple(near, couplings, transfer, cross, coeffs, merged, beside)
    residual, rest = final_lead(near, block_b, rest, lead_b, bases, coupled)
    if line:
        rest = trail_part(near, block_b, rest, inner, early)
        residual = final_trail(near, block_b, rest, (late,), cut, residual)
    else:
        residual = final_trail(near, block_b, rest, trail_b, None, residual)
    return solution_rows, residual


def solution(mesh):
    return jax.shard_map(
        shards,
        mesh=mesh,
        in_specs=(
            P(("group", "member"), None),
            P(("group", "member"), None),
            P(("group", "member"), None),
            P(("group", "member"), None),
            P(("group", "member"), None),
            P(("group", "member"), None, None, None),
            P(("group", "member"), None, None),
            P("group", None, None, None),
            P(),
            P(),
        ),
        out_specs=(P(("group", "member"), None), P(("group", "member"), None)),
        check_vma=False,
    )
```

```python
import math

import jax
import jax.numpy as jnp
from jax import lax
from jax.experimental import pallas as pl
from jax.experimental.pallas import tpu as pltpu
from jax.sharding import PartitionSpec as P


RIDGE = 0.5
KERNEL_WIDTH = 8.0
REACH = 2
F32 = jnp.float32
BF16 = jnp.bfloat16
VMEM = pltpu.VMEM
ANY = pl.ANY


def cycle(array, axis, by):
    count = lax.axis_size(axis)
    return lax.ppermute(array, axis, [(i, (i + by) % count) for i in range(count)])


def tile_of(rows):
    return 512 if rows % 512 == 0 else rows


def over_tiles(rows, body):
    tile = tile_of(rows)

    def step(k, carry):
        body(pl.ds(pl.multiple_of(k * tile, tile), tile))
        return carry

    lax.fori_loop(0, rows // tile, step, 0)


def shape(dtype, *dims):
    return jax.ShapeDtypeStruct(dims, dtype)


SMEM_SPEC = pl.BlockSpec(memory_space=pltpu.SMEM)
ANY_SPEC = pl.BlockSpec(memory_space=ANY)


VMEM_SPEC = pl.BlockSpec(memory_space=VMEM)
HBM_SPEC = pl.BlockSpec(memory_space=pltpu.HBM)


def call(body, out, args, scratch=(), scalars=0, in_specs=None, out_specs=None, flops=0, bytes_=0, exps=0,
         aliases=None):
    many = isinstance(out, tuple)
    return pl.pallas_call(
        body,
        out_shape=out,
        in_specs=in_specs or [SMEM_SPEC] * scalars + [VMEM_SPEC] * (len(args) - scalars),
        out_specs=out_specs or ((VMEM_SPEC,) * len(out) if many else VMEM_SPEC),
        scratch_shapes=list(scratch),
        input_output_aliases=aliases or {},
        cost_estimate=pl.CostEstimate(flops=flops, bytes_accessed=bytes_, transcendentals=exps),
        compiler_params=pltpu.CompilerParams(vmem_limit_bytes=20 * 1024 * 1024),
    )(*args)


def dot(left, right):
    return jnp.dot(left, right, preferred_element_type=F32)


def dot_tn(left, right):
    return lax.dot_general(left, right, (((0,), (0,)), ((), ())), preferred_element_type=F32)


def dot_nt(left, right):
    return lax.dot_general(left, right, (((1,), (1,)), ((), ())), preferred_element_type=F32)


def pieces(value):
    first = value.astype(BF16).astype(F32)
    rest = value - first
    second = rest.astype(BF16).astype(F32)
    return first, second, rest - second


def augmented(block, left):
    rows, dims = block.shape
    wide = block.astype(F32)
    norm = jnp.sum(wide * wide, axis=1, keepdims=True)
    value = -norm / KERNEL_WIDTH
    if left:
        value = value + (dims / 16.0 - math.log(2.0 * rows))
        block = (wide * (2.0 / KERNEL_WIDTH)).astype(BF16)
    lane = lax.broadcasted_iota(jnp.int32, (rows, 128), 1)
    at, ones_at = (0, 3) if left else (3, 0)
    extra = jnp.where((lane >= ones_at) & (lane < ones_at + 3), 1.0, 0.0)
    for k, piece in enumerate(pieces(value)):
        extra = jnp.where(lane == at + k, piece, extra)
    return block, extra.astype(BF16)


def fill_augmented(target, block, left):
    dims = block.shape[1]
    main, extra = augmented(block, left)
    target[:, :dims] = main
    target[:, dims:] = extra


def kernel_tile(left_tile, right_all):
    return jnp.exp(dot_nt(left_tile, right_all)).astype(BF16)


def pick(choice, candidates, use):
    for k, candidate in enumerate(candidates):
        @pl.when(choice == k)
        def _():
            use(candidate)


def paired(members):
    return members == 2 * REACH


def at_end(member, members):
    return (member == 0) | (member == members - 1)


def slots(near_ref, members):
    member = lax.axis_index("member")
    one = near_ref[0, 0] - member
    two = near_ref[0, 1] - member
    if paired(members):
        toward = 1 - 2 * lax.rem(member, 2)
        outer = (one == toward) | (two == toward)
        inner = (one == -toward) | (two == -toward)
        return jnp.where(outer, 0, 1), jnp.where(outer & inner, 0, 1)

    def index(offset):
        return jnp.where(offset == -1, 0, jnp.where(offset == 1, 1, jnp.where(offset == -2, 2, 3)))

    return index(one), index(two)


def with_slot_b(near_ref, members, block_ref, candidates, use):
    choice = slots(near_ref, members)[1]
    for k, ref in enumerate(candidates):
        @pl.when(choice == k)
        def _():
            use(lambda at: dot(block_ref[at, :], ref[...]))


def beside_pair(member, members):
    other = member - 1 if member % 2 == 0 else member + 1
    return other if 0 <= other < members else member


def permute(block, pairs):
    return lax.ppermute(block, "member", pairs)


def mates(members):
    return [(i, i + 1 - 2 * (i % 2)) for i in range(members)]


def hop(block):
    members = lax.axis_size("member")
    inner = permute(block, [(i, beside_pair(i, members)) for i in range(members)])
    return inner, permute(block, mates(members))


def across(inner):
    members = lax.axis_size("member")
    beside = [beside_pair(i, members) for i in range(members)]
    return permute(
        inner, [(i, b + REACH if b + REACH < members else b - REACH) for i, b in enumerate(beside)])


def exchange(block):
    members = lax.axis_size("member")
    up = [(i, i + 1) for i in range(members - 1)]
    down = [(i + 1, i) for i in range(members - 1)]
    before = permute(block, up)
    after = permute(block, down)
    return before, after, permute(before, up), permute(after, down)


def factors(low_ref, high_ref, width):
    low = jnp.broadcast_to(low_ref[...], (1, width))
    high = jnp.broadcast_to(high_ref[...], (1, width))
    theta = (high + low) / 2.0
    delta = (high - low) / 2.0
    sigma = theta / delta
    rho_zero = 1.0 / sigma
    rho_one = 1.0 / (2.0 * sigma - rho_zero)
    return theta, rho_one * rho_zero, 2.0 * rho_one / delta


def start_rows(right_sides, order, low, high):
    rows, width = right_sides.shape
    half = width // 2
    step = tile_of(rows)

    def body(low_ref, high_ref, right_ref, order_ref, lead_ref, trail_ref, turned):
        theta, _, _ = factors(low_ref, high_ref, width)
        turned[...] = (right_ref[...] / theta).astype(BF16).T

        for k in range(rows // step):
            at = pl.ds(k * step, step)
            source = lax.broadcasted_iota(jnp.int32, (rows, step), 0)
            places = jnp.where(source == order_ref[:, at], 1.0, 0.0).astype(BF16)
            v = dot(turned[...], places).T.astype(BF16)
            lead_ref[at, :] = v[:, :half]
            trail_ref[at, :] = v[:, half:]

    return call(
        body, (shape(BF16, rows, half), shape(BF16, rows, width - half)), (low, high, right_sides, order),
        scratch=[VMEM((width, rows), BF16)],
        flops=2 * rows * rows * width, bytes_=rows * width * 6,
    )


def order_rows(right_sides, order):
    rows, width = right_sides.shape
    step = tile_of(rows)

    def body(right_ref, order_ref, out_ref, turned):
        for k, piece in enumerate(pieces(right_ref[...])):
            turned[k * width : (k + 1) * width, :] = piece.astype(BF16).T

        for k in range(rows // step):
            at = pl.ds(k * step, step)
            source = lax.broadcasted_iota(jnp.int32, (rows, step), 0)
            places = jnp.where(source == order_ref[:, at], 1.0, 0.0).astype(BF16)
            v = dot(turned[...], places)
            out_ref[at, :] = (v[:width] + v[width : 2 * width] + v[2 * width :]).T

    return call(
        body, shape(F32, rows, width), (right_sides, order), scratch=[VMEM((3 * width, rows), BF16)],
        flops=6 * rows * rows * width, bytes_=rows * width * 8,
    )


def start_message(lead, trail, bases, transfer):
    rows, half = lead.shape
    rank = bases.shape[1]
    width = half + trail.shape[1]

    def body(lead_ref, trail_ref, bases_ref, transfer_ref, message_ref, v):
        join(lead_ref, trail_ref, v)
        message_ref[:, :width] = dot_tn(bases_ref[...], v[...]).astype(BF16)
        message_ref[:, width:] = transfer_ref[...]

    return call(
        body, shape(BF16, rank, width + rank), (lead, trail, bases, transfer),
        scratch=[VMEM((rows, width), BF16)],
        flops=2 * rows * width * rank, bytes_=rows * width * 2 + rows * rank * 2,
    )


def join(lead_ref, trail_ref, target):
    half = trail_ref.shape[1]
    target[:, :half] = lead_ref[...]
    target[:, half:] = trail_ref[...]


def self_first(points, ordered, lead, trail, low, high):
    rows, width = ordered.shape
    dims = points.shape[1]

    def body(low_ref, high_ref, points_ref, ordered_ref, lead_ref, trail_ref, block_ref, rest_ref,
             left, right, v):
        theta, _, _ = factors(low_ref, high_ref, width)
        join(lead_ref, trail_ref, v)
        fill_augmented(left, points_ref[...], True)
        fill_augmented(right, points_ref[...], False)

        def tile(at):
            block = kernel_tile(left[at, :], right[...])
            block_ref[at, :] = block
            own = ordered_ref[at, :]
            rest_ref[at, :] = own - RIDGE * (own / theta) - dot(block, v[...])

        over_tiles(rows, tile)

    return call(
        body, (shape(BF16, rows, rows), shape(F32, rows, width)),
        (low, high, points, ordered, lead, trail),
        scratch=[VMEM((rows, dims + 128), BF16), VMEM((rows, dims + 128), BF16), VMEM((rows, width), BF16)],
        flops=2 * rows * rows * (width + dims), bytes_=rows * rows * 2 + rows * width * 10,
        exps=rows * rows,
    )


def near_block(which, near, points, candidates):
    rows, dims = points.shape
    members = lax.axis_size("member")
    count = len(candidates)

    def body(near_ref, points_ref, *rest):
        others, (block_ref, left, right) = rest[:count], rest[count:]
        fill_augmented(left, points_ref[...], True)
        pick(slots(near_ref, members)[which], others,
             lambda points_of: fill_augmented(right, points_of[...], False))

        def tile(at):
            block_ref[at, :] = kernel_tile(left[at, :], right[...])

        over_tiles(rows, tile)

    return call(
        body, shape(BF16, rows, rows), (near, points, *candidates), scalars=1,
        scratch=[VMEM((rows, dims + 128), BF16), VMEM((rows, dims + 128), BF16)],
        flops=2 * rows * rows * dims, bytes_=rows * rows * 2 + rows * dims * 4, exps=rows * rows,
    )


def subtract_near(near, block, rest, leads, trails):
    rows, width = rest.shape
    members = lax.axis_size("member")
    count = len(leads)

    def body(near_ref, block_ref, rest_ref, *refs):
        pairs = list(zip(refs[:count], refs[count : 2 * count]))
        out_ref, v = refs[2 * count :]
        pick(slots(near_ref, members)[0], pairs, lambda pair: join(*pair, v))

        def tile(at):
            out_ref[at, :] = rest_ref[at, :] - dot(block_ref[at, :], v[...])

        over_tiles(rows, tile)

    return call(
        body, shape(F32, rows, width), (near, block, rest, *leads, *trails), scalars=1,
        scratch=[VMEM((rows, width), BF16)],
        flops=2 * rows * rows * width, bytes_=rows * rows * 2 + rows * width * 10,
    )


def turn(column, near, block, rest, candidates, bases, coupled, ordered, low, high, joined=()):
    rows, width = rest.shape
    rank = bases.shape[1]
    half = width // 2
    members = lax.axis_size("member")
    count = len(candidates)
    kept = len(joined)
    columns = slice(column * half, (column + 1) * half)

    def body(near_ref, low_ref, high_ref, block_ref, rest_ref, bases_ref, coupled_ref, ordered_ref, *refs):
        others, joined_refs = refs[:count], refs[count : count + kept]
        first_ref, v_ref, coeff_ref, total = refs[count + kept :]
        theta, keep, push = factors(low_ref, high_ref, half)
        total[...] = jnp.zeros_like(total)

        def use(slot_b):
            def tile(at):
                own = bases_ref[at, :]
                first = rest_ref[at, columns] - slot_b(at) - dot(own, coupled_ref[:, columns])
                first_ref[at, :] = first
                moved = (keep * (ordered_ref[at, columns] / theta) + push * first).astype(BF16)
                v_ref[at, :] = moved
                total[...] += dot_tn(own, moved)

            over_tiles(rows, tile)

        with_slot_b(near_ref, members, block_ref, others, use)
        for joined_ref in joined_refs:
            coeff_ref[:, :half] = joined_ref[...]
        coeff_ref[:, kept * half :] = total[...].astype(BF16)

    return call(
        body,
        (shape(F32, rows, half), shape(BF16, rows, half), shape(BF16, rank, half * (kept + 1))),
        (near, low, high, block, rest, bases, coupled, ordered, *candidates, *joined), scalars=1,
        scratch=[VMEM((rank, half), F32)],
        flops=2 * rows * rows * half, bytes_=rows * rows * 2 + rows * half * 16,
    )


def self_second(block, lead, trail, first_lead, first_trail, ordered, low, high):
    rows, width = ordered.shape
    half = width // 2

    def body(low_ref, high_ref, block_ref, lead_ref, trail_ref, first_lead_ref, first_trail_ref, ordered_ref,
             solution_ref, rest_ref, v):
        join(lead_ref, trail_ref, v)
        theta, keep, push = factors(low_ref, high_ref, half)

        def tile(at):
            product = dot(block_ref[at, :], v[...])
            for k, ref in enumerate((first_lead_ref, first_trail_ref)):
                columns = slice(k * half, (k + 1) * half)
                first = ref[at, :]
                step_zero = ordered_ref[at, columns] / theta
                step_one = keep * step_zero + push * first
                solution_ref[at, columns] = step_zero + step_one
                rest_ref[at, columns] = first - RIDGE * step_one - product[:, columns]

        over_tiles(rows, tile)

    return call(
        body, (shape(F32, rows, width), shape(F32, rows, width)),
        (low, high, block, lead, trail, first_lead, first_trail, ordered),
        scratch=[VMEM((rows, width), BF16)],
        flops=2 * rows * rows * width, bytes_=rows * rows * 2 + rows * width * 18,
    )


def write_tiles(steps, tile, result, out_ref, columns, sems):
    copies = []
    for k, (first, count) in enumerate(steps):
        at = pl.ds(first, count)
        result[at, :] = tile(at)
        copies.append(pltpu.make_async_copy(result.at[at, :], out_ref.at[at, columns], sems.at[k]))
        copies[-1].start()
    for started in copies:
        started.wait()


def final_lead(near, block, rest, candidates, bases, coupled):
    rows, width = rest.shape
    half = width // 2
    members = lax.axis_size("member")
    count = len(candidates)
    tile_rows = tile_of(rows)
    steps = [(k, tile_rows) for k in range(0, rows, tile_rows)]

    def body(near_ref, block_ref, rest_ref, bases_ref, coupled_ref, *refs):
        others, (out_ref, trail_ref, result, sems) = refs[:count], refs[count:]

        def use(slot_b):
            def tile(at):
                other = rest_ref[at, :] - dot(bases_ref[at, :], coupled_ref[...])
                trail_ref[at, :] = other[:, half:]
                return other[:, :half] - slot_b(at)

            write_tiles(steps, tile, result, out_ref, pl.ds(0, half), sems)

        with_slot_b(near_ref, members, block_ref, others, use)

    return call(
        body, (shape(F32, rows, width), shape(F32, rows, half)),
        (near, block, rest, bases, coupled, *candidates), scalars=1, out_specs=(ANY_SPEC, VMEM_SPEC),
        scratch=[VMEM((rows, half), F32), pltpu.SemaphoreType.DMA((len(steps),))],
        flops=2 * rows * rows * half, bytes_=rows * rows * 2 + rows * half * 10,
    )


def trail_part(near, block, trail, inner, piece):
    rows, half = trail.shape
    members = lax.axis_size("member")
    cut = piece.shape[0]

    def body(near_ref, block_ref, trail_ref, inner_ref, piece_ref, out_ref):
        choice = slots(near_ref, members)[1]

        @pl.when(choice == 0)
        def _():
            def tile(at):
                out_ref[at, :] = trail_ref[at, :] - dot(block_ref[at, :], inner_ref[...])

            over_tiles(rows, tile)

        @pl.when(choice != 0)
        def _():
            def tile(at):
                out_ref[at, :] = trail_ref[at, :] - dot(block_ref[at, :cut], piece_ref[...])

            over_tiles(rows, tile)

    return call(
        body, shape(F32, rows, half), (near, block, trail, inner, piece), scalars=1,
        flops=2 * rows * cut * half, bytes_=rows * cut * 2 + rows * half * 8,
    )


def final_trail(near, block, trail, candidates, first, written):
    rows, half = trail.shape
    members = lax.axis_size("member")
    count = len(candidates)
    tile_rows = tile_of(rows)
    steps = [(k, tile_rows) for k in range(0, rows, tile_rows)]

    def body(near_ref, block_ref, trail_ref, *refs):
        others, (out_ref, result, sems) = refs[:count], refs[-3:]

        def use(slot_b):
            def tile(at):
                return trail_ref[at, :] - slot_b(at)

            write_tiles(steps, tile, result, out_ref, pl.ds(half, half), sems)

        if first is None:
            with_slot_b(near_ref, members, block_ref, others, use)
        else:
            late = slots(near_ref, members)[1] != 0
            pl.when(late)(lambda: use(lambda at: dot(block_ref[at, first:], others[0][...])))
            pl.when(jnp.logical_not(late))(lambda: use(lambda at: 0.0))

    return call(
        body, shape(F32, *written.shape), (near, block, trail, *candidates, written),
        in_specs=[SMEM_SPEC] + [VMEM_SPEC] * (2 + count) + [ANY_SPEC], out_specs=ANY_SPEC,
        scratch=[VMEM((rows, half), F32), pltpu.SemaphoreType.DMA((len(steps),))],
        flops=2 * rows * rows * half, bytes_=rows * rows * 2 + rows * half * 10,
        aliases={3 + count: 0},
    )


def merge_all(message, first, rank):
    members = lax.axis_size("member")
    width = first["own"].shape[1] - rank if first else message.shape[1] - rank
    if not paired(members):
        others = around(message, "member")
        state = {"own": message, "others": others}
        first = first or state
        merged = merge_ring(state, first, rank, width)
        return state, merged
    down = mates(members)
    up = mates(members)
    mate = permute(message, down)
    pair = pack((message, mate))
    crossed = permute(pair, [(i, beside_pair(i, members)) for i in range(members)])
    state = {"own": message, "pair": pair, "crossed": crossed}
    first = first or state
    summed = merge_line(state, first, rank, width)
    handed = permute(summed, up)
    state["handed"] = handed
    return state, choose(summed, handed, width)


def merge_ring(state, first, rank, width):
    count = len(state["others"]) + 1

    def body(*refs):
        total = jnp.zeros((rank, width), F32)
        for coeff, carried in zip(refs[:count], refs[count:-1]):
            total = total + dot_tn(carried[:, width:], coeff[:, :width])
        refs[-1][...] = total.astype(BF16)

    args = (state["own"], *state["others"], first["own"], *first["others"])
    return call(
        body, shape(BF16, rank, width), args,
        flops=2 * rank * rank * width * count, bytes_=rank * width * 4 * count,
    )


def merge_line(state, first, rank, width):
    def body(pair_ref, crossed_ref, first_pair_ref, first_crossed_ref, out_ref):
        total = jnp.zeros((rank, width), F32)
        for coeffs, carried in ((pair_ref, first_pair_ref), (crossed_ref, first_crossed_ref)):
            for rows in (slice(0, rank), slice(rank, 2 * rank)):
                total = total + dot_tn(carried[rows, width:], coeffs[rows, :width])
        out_ref[:, :width] = total.astype(BF16)
        out_ref[:, width:] = crossed_ref[rank:, :width]

    return call(
        body, shape(BF16, rank, 2 * width),
        (state["pair"], state["crossed"], first["pair"], first["crossed"]),
        flops=8 * rank * rank * width, bytes_=rank * width * 16,
    )


def choose(summed, handed, width):
    members = lax.axis_size("member")

    def body(summed_ref, handed_ref, out_ref):
        end = at_end(lax.axis_index("member"), members)
        out_ref[...] = jnp.where(end, handed_ref[:, :width], summed_ref[:, :width])

    return call(
        body, shape(BF16, summed.shape[0], width), (summed, handed),
        bytes_=summed.shape[0] * width * 6,
    )


def coupled_arrays(state):
    if "others" in state:
        return tuple(state["others"])
    return state["pair"], state["crossed"], state["handed"]


def coupled_views(refs, rank, width):
    members = lax.axis_size("member")
    member = lax.axis_index("member")
    if not paired(members):
        return [(lax.rem(member + (members - 1 - k), members), ref[:, :width]) for k, ref in enumerate(refs)]
    pair_ref, crossed_ref, handed_ref = refs
    lower = member < members // 2
    far_end = jnp.where(lower, members - 1, 0)
    far_middle = jnp.where(lower, members // 2, members // 2 - 1)
    own_end = members - 1 - far_end
    end = at_end(member, members)
    from_far_end = jnp.where(end, handed_ref[:, width:], crossed_ref[rank:, :width])
    return [
        (jnp.where(end, far_middle, own_end), pair_ref[rank:, :width]),
        (far_middle, crossed_ref[:rank, :width]),
        (far_end, from_far_end),
    ]


def pack(blocks):
    rank, width = blocks[0].shape

    def body(*refs):
        for k, ref in enumerate(refs[:-1]):
            refs[-1][k * rank : (k + 1) * rank, :] = ref[...]

    return call(
        body, shape(BF16, rank * len(blocks), width), blocks,
        bytes_=rank * width * 4 * len(blocks),
    )


def inner_of(groups):
    return 2 if groups % 2 == 0 else 1


def all_merged(merged):
    groups = lax.axis_size("group")
    inner = inner_of(groups)
    moved = []
    for k in range(1, groups // inner):
        moved.append(cycle(merged, "group", k * inner))
    if inner == 1:
        return moved, None
    packed = pack((merged, *moved))
    beside = lax.ppermute(packed, "group", [(g, g + 1 - 2 * (g % 2)) for g in range(groups)])
    return moved, beside


def couple(near, couplings, transfer, cross, messages, merged, beside):
    rank = transfer.shape[0]
    width = merged[0].shape[1]
    members = lax.axis_size("member")
    groups = lax.axis_size("group")
    inner = inner_of(groups)
    packed = () if beside is None else (beside,)

    arrays = coupled_arrays(messages)
    count = len(arrays)

    def body(near_ref, couplings_ref, transfer_ref, cross_ref, *refs):
        coeffs, others, out_ref = refs[:count], refs[count:-1], refs[-1]
        group = lax.axis_index("group")
        crossed = jnp.zeros((rank, width), F32)
        for k in range(1, groups // inner):
            source = lax.rem(group + (groups - k * inner), groups)
            crossed = crossed + dot(cross_ref[source], others[k - 1][...])
        if packed:
            side = group + 1 - 2 * lax.rem(group, 2)
            for k in range(groups // inner):
                source = lax.rem(side + (groups - k * inner), groups)
                crossed = crossed + dot(cross_ref[source], others[-1][k * rank : (k + 1) * rank, :])
        within = dot(transfer_ref[...], crossed.astype(BF16))
        for source, coeff in coupled_views(coeffs, rank, width):
            far = (source != near_ref[0, 0]) & (source != near_ref[0, 1])
            within = within + jnp.where(far, 1.0, 0.0) * dot(couplings_ref[source], coeff)
        out_ref[...] = within.astype(BF16)

    args = (near, couplings, transfer, cross, *arrays, *merged, *packed)
    return call(
        body, shape(BF16, rank, width), args, scalars=1,
        flops=2 * rank * rank * width * (members + groups), bytes_=rank * width * 2 * (members + groups) * 2,
    )


def around(array, axis):
    moved = []
    for k in range(1, lax.axis_size(axis)):
        moved.append(cycle(array, axis, k))
    return moved


def shards(
    points,
    right_sides,
    leaf_order,
    near_leaves,
    bases,
    couplings,
    transfers,
    cross_couplings,
    low_bound,
    high_bound,
):
    transfer = transfers[0]
    couplings = couplings[0]
    cross = cross_couplings[0]
    near = near_leaves
    low, high = low_bound.reshape(1, 1), high_bound.reshape(1, 1)

    line = paired(lax.axis_size("member"))

    def moved(block):
        if not line:
            blocks = exchange(block)
            return blocks, blocks
        inner, outer = hop(block)
        return (outer, inner), (inner, across(inner))

    points_a, points_b = moved(points)
    block_a = near_block(0, near, points, points_a)
    block_b = near_block(1, near, points, points_b)
    lead, trail = start_rows(right_sides, leaf_order, low, high)
    ordered = order_rows(right_sides, leaf_order)
    message = start_message(lead, trail, bases, transfer)
    rank = transfer.shape[0]
    messages, merged = merge_all(message, None, rank)
    lead_a, lead_b = moved(lead)
    trail_a, trail_b = moved(trail)
    own_block, rest = self_first(points, ordered, lead, trail, low, high)
    merged, beside = all_merged(merged)
    rest = subtract_near(near, block_a, rest, lead_a, trail_a)
    coupled = couple(near, couplings, transfer, cross, messages, merged, beside)
    first_lead, lead, coeff = turn(0, near, block_b, rest, lead_b, bases, coupled, ordered, low, high)
    first_trail, trail, coeff = turn(
        1, near, block_b, rest, trail_b, bases, coupled, ordered, low, high, (coeff,))

    coeffs, merged = merge_all(coeff, messages, rank)
    lead_a, lead_b = moved(lead)
    if line:
        inner, outer = hop(trail)
        trail_a = (outer, inner)
        cut = 2 * trail.shape[0] // 3 if trail.shape[0] % 384 == 0 else trail.shape[0] // 2
        early = across(inner[:cut])
        late = across(inner[cut:])
    else:
        trail_a, trail_b = moved(trail)
    solution_rows, rest = self_second(own_block, lead, trail, first_lead, first_trail, ordered, low, high)
    merged, beside = all_merged(merged)
    rest = subtract_near(near, block_a, rest, lead_a, trail_a)
    coupled = couple(near, couplings, transfer, cross, coeffs, merged, beside)
    residual, rest = final_lead(near, block_b, rest, lead_b, bases, coupled)
    if line:
        rest = trail_part(near, block_b, rest, inner, early)
        residual = final_trail(near, block_b, rest, (late,), cut, residual)
    else:
        residual = final_trail(near, block_b, rest, trail_b, None, residual)
    return solution_rows, residual


def solution(mesh):
    return jax.shard_map(
        shards,
        mesh=mesh,
        in_specs=(
            P(("group", "member"), None),
            P(("group", "member"), None),
            P(("group", "member"), None),
            P(("group", "member"), None),
            P(("group", "member"), None),
            P(("group", "member"), None, None, None),
            P(("group", "member"), None, None),
            P("group", None, None, None),
            P(),
            P(),
        ),
        out_specs=(P(("group", "member"), None), P(("group", "member"), None)),
        check_vma=False,
    )
```

```python
import math

import jax
import jax.numpy as jnp
from jax import lax
from jax.experimental import pallas as pl
from jax.experimental.pallas import tpu as pltpu
from jax.sharding import PartitionSpec as P


RIDGE = 0.5
KERNEL_WIDTH = 8.0
REACH = 2
F32 = jnp.float32
BF16 = jnp.bfloat16
VMEM = pltpu.VMEM
ANY = pl.ANY


def cycle(array, axis, by):
    count = lax.axis_size(axis)
    return lax.ppermute(array, axis, [(i, (i + by) % count) for i in range(count)])


def tile_of(rows):
    return 512 if rows % 512 == 0 else rows


def over_tiles(rows, body):
    tile = tile_of(rows)

    def step(k, carry):
        body(pl.ds(pl.multiple_of(k * tile, tile), tile))
        return carry

    lax.fori_loop(0, rows // tile, step, 0)


def shape(dtype, *dims):
    return jax.ShapeDtypeStruct(dims, dtype)


SMEM_SPEC = pl.BlockSpec(memory_space=pltpu.SMEM)
ANY_SPEC = pl.BlockSpec(memory_space=ANY)


VMEM_SPEC = pl.BlockSpec(memory_space=VMEM)
HBM_SPEC = pl.BlockSpec(memory_space=pltpu.HBM)


def call(body, out, args, scratch=(), scalars=0, in_specs=None, out_specs=None, flops=0, bytes_=0, exps=0,
         aliases=None):
    many = isinstance(out, tuple)
    return pl.pallas_call(
        body,
        out_shape=out,
        in_specs=in_specs or [SMEM_SPEC] * scalars + [VMEM_SPEC] * (len(args) - scalars),
        out_specs=out_specs or ((VMEM_SPEC,) * len(out) if many else VMEM_SPEC),
        scratch_shapes=list(scratch),
        input_output_aliases=aliases or {},
        cost_estimate=pl.CostEstimate(flops=flops, bytes_accessed=bytes_, transcendentals=exps),
        compiler_params=pltpu.CompilerParams(vmem_limit_bytes=20 * 1024 * 1024),
    )(*args)


def dot(left, right):
    return jnp.dot(left, right, preferred_element_type=F32)


def dot_tn(left, right):
    return lax.dot_general(left, right, (((0,), (0,)), ((), ())), preferred_element_type=F32)


def dot_nt(left, right):
    return lax.dot_general(left, right, (((1,), (1,)), ((), ())), preferred_element_type=F32)


def pieces(value):
    first = value.astype(BF16).astype(F32)
    rest = value - first
    second = rest.astype(BF16).astype(F32)
    return first, second, rest - second


def augmented(block, left):
    rows, dims = block.shape
    wide = block.astype(F32)
    norm = jnp.sum(wide * wide, axis=1, keepdims=True)
    value = -norm / KERNEL_WIDTH
    if left:
        value = value + (dims / 16.0 - math.log(2.0 * rows))
        block = (wide * (2.0 / KERNEL_WIDTH)).astype(BF16)
    lane = lax.broadcasted_iota(jnp.int32, (rows, 128), 1)
    at, ones_at = (0, 3) if left else (3, 0)
    extra = jnp.where((lane >= ones_at) & (lane < ones_at + 3), 1.0, 0.0)
    for k, piece in enumerate(pieces(value)):
        extra = jnp.where(lane == at + k, piece, extra)
    return block, extra.astype(BF16)


def fill_augmented(target, block, left):
    dims = block.shape[1]
    main, extra = augmented(block, left)
    target[:, :dims] = main
    target[:, dims:] = extra


def kernel_tile(left_tile, right_all):
    return jnp.exp(dot_nt(left_tile, right_all)).astype(BF16)


def pick(choice, candidates, use):
    for k, candidate in enumerate(candidates):
        @pl.when(choice == k)
        def _():
            use(candidate)


def paired(members):
    return members == 2 * REACH


def at_end(member, members):
    return (member == 0) | (member == members - 1)


def slots(near_ref, members):
    member = lax.axis_index("member")
    one = near_ref[0, 0] - member
    two = near_ref[0, 1] - member
    if paired(members):
        toward = 1 - 2 * lax.rem(member, 2)
        outer = (one == toward) | (two == toward)
        inner = (one == -toward) | (two == -toward)
        return jnp.where(outer, 0, 1), jnp.where(outer & inner, 0, 1)

    def index(offset):
        return jnp.where(offset == -1, 0, jnp.where(offset == 1, 1, jnp.where(offset == -2, 2, 3)))

    return index(one), index(two)


def with_slot_b(near_ref, members, block_ref, candidates, use):
    choice = slots(near_ref, members)[1]
    for k, ref in enumerate(candidates):
        @pl.when(choice == k)
        def _():
            use(lambda at: dot(block_ref[at, :], ref[...]))


def beside_pair(member, members):
    other = member - 1 if member % 2 == 0 else member + 1
    return other if 0 <= other < members else member


def permute(block, pairs):
    return lax.ppermute(block, "member", pairs)


def mates(members):
    return [(i, i + 1 - 2 * (i % 2)) for i in range(members)]


def hop(block):
    members = lax.axis_size("member")
    inner = permute(block, [(i, beside_pair(i, members)) for i in range(members)])
    return inner, permute(block, mates(members))


def across(inner):
    members = lax.axis_size("member")
    beside = [beside_pair(i, members) for i in range(members)]
    return permute(
        inner, [(i, b + REACH if b + REACH < members else b - REACH) for i, b in enumerate(beside)])


def exchange(block):
    members = lax.axis_size("member")
    up = [(i, i + 1) for i in range(members - 1)]
    down = [(i + 1, i) for i in range(members - 1)]
    before = permute(block, up)
    after = permute(block, down)
    return before, after, permute(before, up), permute(after, down)


def factors(low_ref, high_ref, width):
    low = jnp.broadcast_to(low_ref[...], (1, width))
    high = jnp.broadcast_to(high_ref[...], (1, width))
    theta = (high + low) / 2.0
    delta = (high - low) / 2.0
    sigma = theta / delta
    rho_zero = 1.0 / sigma
    rho_one = 1.0 / (2.0 * sigma - rho_zero)
    return theta, rho_one * rho_zero, 2.0 * rho_one / delta


def start_rows(right_sides, order, low, high):
    rows, width = right_sides.shape
    half = width // 2
    step = tile_of(rows)

    def body(low_ref, high_ref, right_hbm, order_hbm, lead_ref, trail_ref, right, order, turned, sems):
        theta, _, _ = factors(low_ref, high_ref, width)
        tiles = [pl.ds(k * step, step) for k in range(rows // step)]
        copies = [pltpu.make_async_copy(right_hbm.at[at, :], right.at[at, :], sems.at[k])
                  for k, at in enumerate(tiles)]
        copies.append(pltpu.make_async_copy(order_hbm, order, sems.at[len(tiles)]))
        for copy in copies:
            copy.start()
        for copy, at in zip(copies, tiles):
            copy.wait()
            turned[:, at] = (right[at, :] / theta).astype(BF16).T
        copies[-1].wait()
        for at in tiles:
            source = lax.broadcasted_iota(jnp.int32, (rows, step), 0)
            places = jnp.where(source == order[:, at], 1.0, 0.0).astype(BF16)
            v = dot(turned[...], places).T.astype(BF16)
            lead_ref[at, :] = v[:, :half]
            trail_ref[at, :] = v[:, half:]

    return call(
        body, (shape(BF16, rows, half), shape(BF16, rows, width - half)),
        (low, high, pltpu.with_memory_space_constraint(right_sides, pltpu.HBM),
         pltpu.with_memory_space_constraint(order, pltpu.HBM)),
        in_specs=[VMEM_SPEC, VMEM_SPEC, HBM_SPEC, HBM_SPEC],
        scratch=[VMEM((rows, width), F32), VMEM((1, rows), jnp.int32), VMEM((width, rows), BF16),
                 pltpu.SemaphoreType.DMA((rows // step + 1,))],
        flops=2 * rows * rows * width, bytes_=rows * width * 6,
    )


def order_rows(right_sides, order):
    rows, width = right_sides.shape
    step = tile_of(rows)

    def body(right_ref, order_ref, out_ref, turned):
        for k, piece in enumerate(pieces(right_ref[...])):
            turned[k * width : (k + 1) * width, :] = piece.astype(BF16).T

        for k in range(rows // step):
            at = pl.ds(k * step, step)
            source = lax.broadcasted_iota(jnp.int32, (rows, step), 0)
            places = jnp.where(source == order_ref[:, at], 1.0, 0.0).astype(BF16)
            v = dot(turned[...], places)
            out_ref[at, :] = (v[:width] + v[width : 2 * width] + v[2 * width :]).T

    return call(
        body, shape(F32, rows, width), (right_sides, order), scratch=[VMEM((3 * width, rows), BF16)],
        flops=6 * rows * rows * width, bytes_=rows * width * 8,
    )


def start_message(lead, trail, bases, transfer):
    rows, half = lead.shape
    rank = bases.shape[1]
    width = half + trail.shape[1]

    def body(lead_ref, trail_ref, bases_ref, transfer_ref, message_ref, v):
        join(lead_ref, trail_ref, v)
        message_ref[:, :width] = dot_tn(bases_ref[...], v[...]).astype(BF16)
        message_ref[:, width:] = transfer_ref[...]

    return call(
        body, shape(BF16, rank, width + rank), (lead, trail, bases, transfer),
        scratch=[VMEM((rows, width), BF16)],
        flops=2 * rows * width * rank, bytes_=rows * width * 2 + rows * rank * 2,
    )


def join(lead_ref, trail_ref, target):
    half = trail_ref.shape[1]
    target[:, :half] = lead_ref[...]
    target[:, half:] = trail_ref[...]


def self_first(points, ordered, lead, trail, low, high):
    rows, width = ordered.shape
    dims = points.shape[1]

    def body(low_ref, high_ref, points_ref, ordered_ref, lead_ref, trail_ref, block_ref, rest_ref,
             left, right, v):
        theta, _, _ = factors(low_ref, high_ref, width)
        join(lead_ref, trail_ref, v)
        fill_augmented(left, points_ref[...], True)
        fill_augmented(right, points_ref[...], False)

        def tile(at):
            block = kernel_tile(left[at, :], right[...])
            block_ref[at, :] = block
            own = ordered_ref[at, :]
            rest_ref[at, :] = own - RIDGE * (own / theta) - dot(block, v[...])

        over_tiles(rows, tile)

    return call(
        body, (shape(BF16, rows, rows), shape(F32, rows, width)),
        (low, high, points, ordered, lead, trail),
        scratch=[VMEM((rows, dims + 128), BF16), VMEM((rows, dims + 128), BF16), VMEM((rows, width), BF16)],
        flops=2 * rows * rows * (width + dims), bytes_=rows * rows * 2 + rows * width * 10,
        exps=rows * rows,
    )


def near_block(which, near, points, candidates):
    rows, dims = points.shape
    members = lax.axis_size("member")
    count = len(candidates)

    def body(near_ref, points_ref, *rest):
        others, (block_ref, left, right) = rest[:count], rest[count:]
        fill_augmented(left, points_ref[...], True)
        pick(slots(near_ref, members)[which], others,
             lambda points_of: fill_augmented(right, points_of[...], False))

        def tile(at):
            block_ref[at, :] = kernel_tile(left[at, :], right[...])

        over_tiles(rows, tile)

    return call(
        body, shape(BF16, rows, rows), (near, points, *candidates), scalars=1,
        scratch=[VMEM((rows, dims + 128), BF16), VMEM((rows, dims + 128), BF16)],
        flops=2 * rows * rows * dims, bytes_=rows * rows * 2 + rows * dims * 4, exps=rows * rows,
    )


def subtract_near(near, block, rest, leads, trails):
    rows, width = rest.shape
    members = lax.axis_size("member")
    count = len(leads)

    def body(near_ref, block_ref, rest_ref, *refs):
        pairs = list(zip(refs[:count], refs[count : 2 * count]))
        out_ref, v = refs[2 * count :]
        pick(slots(near_ref, members)[0], pairs, lambda pair: join(*pair, v))

        def tile(at):
            out_ref[at, :] = rest_ref[at, :] - dot(block_ref[at, :], v[...])

        over_tiles(rows, tile)

    return call(
        body, shape(F32, rows, width), (near, block, rest, *leads, *trails), scalars=1,
        scratch=[VMEM((rows, width), BF16)],
        flops=2 * rows * rows * width, bytes_=rows * rows * 2 + rows * width * 10,
    )


def turn(column, near, block, rest, candidates, bases, coupled, ordered, low, high, joined=()):
    rows, width = rest.shape
    rank = bases.shape[1]
    half = width // 2
    members = lax.axis_size("member")
    count = len(candidates)
    kept = len(joined)
    columns = slice(column * half, (column + 1) * half)

    def body(near_ref, low_ref, high_ref, block_ref, rest_ref, bases_ref, coupled_ref, ordered_ref, *refs):
        others, joined_refs = refs[:count], refs[count : count + kept]
        first_ref, v_ref, coeff_ref, total = refs[count + kept :]
        theta, keep, push = factors(low_ref, high_ref, half)
        total[...] = jnp.zeros_like(total)

        def use(slot_b):
            def tile(at):
                own = bases_ref[at, :]
                first = rest_ref[at, columns] - slot_b(at) - dot(own, coupled_ref[:, columns])
                first_ref[at, :] = first
                moved = (keep * (ordered_ref[at, columns] / theta) + push * first).astype(BF16)
                v_ref[at, :] = moved
                total[...] += dot_tn(own, moved)

            over_tiles(rows, tile)

        with_slot_b(near_ref, members, block_ref, others, use)
        for joined_ref in joined_refs:
            coeff_ref[:, :half] = joined_ref[...]
        coeff_ref[:, kept * half :] = total[...].astype(BF16)

    return call(
        body,
        (shape(F32, rows, half), shape(BF16, rows, half), shape(BF16, rank, half * (kept + 1))),
        (near, low, high, block, rest, bases, coupled, ordered, *candidates, *joined), scalars=1,
        scratch=[VMEM((rank, half), F32)],
        flops=2 * rows * rows * half, bytes_=rows * rows * 2 + rows * half * 16,
    )


def self_second(block, lead, trail, first_lead, first_trail, ordered, low, high):
    rows, width = ordered.shape
    half = width // 2

    def body(low_ref, high_ref, block_ref, lead_ref, trail_ref, first_lead_ref, first_trail_ref, ordered_ref,
             solution_ref, rest_ref, v):
        join(lead_ref, trail_ref, v)
        theta, keep, push = factors(low_ref, high_ref, half)

        def tile(at):
            product = dot(block_ref[at, :], v[...])
            for k, ref in enumerate((first_lead_ref, first_trail_ref)):
                columns = slice(k * half, (k + 1) * half)
                first = ref[at, :]
                step_zero = ordered_ref[at, columns] / theta
                step_one = keep * step_zero + push * first
                solution_ref[at, columns] = step_zero + step_one
                rest_ref[at, columns] = first - RIDGE * step_one - product[:, columns]

        over_tiles(rows, tile)

    return call(
        body, (shape(F32, rows, width), shape(F32, rows, width)),
        (low, high, block, lead, trail, first_lead, first_trail, ordered),
        scratch=[VMEM((rows, width), BF16)],
        flops=2 * rows * rows * width, bytes_=rows * rows * 2 + rows * width * 18,
    )


def write_tiles(steps, tile, result, out_ref, columns, sems):
    copies = []
    for k, (first, count) in enumerate(steps):
        at = pl.ds(first, count)
        result[at, :] = tile(at)
        copies.append(pltpu.make_async_copy(result.at[at, :], out_ref.at[at, columns], sems.at[k]))
        copies[-1].start()
    for started in copies:
        started.wait()


def final_lead(near, block, rest, candidates, bases, coupled):
    rows, width = rest.shape
    half = width // 2
    members = lax.axis_size("member")
    count = len(candidates)
    tile_rows = tile_of(rows)
    steps = [(k, tile_rows) for k in range(0, rows, tile_rows)]

    def body(near_ref, block_ref, rest_ref, bases_ref, coupled_ref, *refs):
        others, (out_ref, trail_ref, result, sems) = refs[:count], refs[count:]

        def use(slot_b):
            def tile(at):
                other = rest_ref[at, :] - dot(bases_ref[at, :], coupled_ref[...])
                trail_ref[at, :] = other[:, half:]
                return other[:, :half] - slot_b(at)

            write_tiles(steps, tile, result, out_ref, pl.ds(0, half), sems)

        with_slot_b(near_ref, members, block_ref, others, use)

    return call(
        body, (shape(F32, rows, width), shape(F32, rows, half)),
        (near, block, rest, bases, coupled, *candidates), scalars=1, out_specs=(ANY_SPEC, VMEM_SPEC),
        scratch=[VMEM((rows, half), F32), pltpu.SemaphoreType.DMA((len(steps),))],
        flops=2 * rows * rows * half, bytes_=rows * rows * 2 + rows * half * 10,
    )


def trail_part(near, block, trail, inner, piece):
    rows, half = trail.shape
    members = lax.axis_size("member")
    cut = piece.shape[0]

    def body(near_ref, block_ref, trail_ref, inner_ref, piece_ref, out_ref):
        choice = slots(near_ref, members)[1]

        @pl.when(choice == 0)
        def _():
            def tile(at):
                out_ref[at, :] = trail_ref[at, :] - dot(block_ref[at, :], inner_ref[...])

            over_tiles(rows, tile)

        @pl.when(choice != 0)
        def _():
            def tile(at):
                out_ref[at, :] = trail_ref[at, :] - dot(block_ref[at, :cut], piece_ref[...])

            over_tiles(rows, tile)

    return call(
        body, shape(F32, rows, half), (near, block, trail, inner, piece), scalars=1,
        flops=2 * rows * cut * half, bytes_=rows * cut * 2 + rows * half * 8,
    )


def final_trail(near, block, trail, candidates, first, written):
    rows, half = trail.shape
    members = lax.axis_size("member")
    count = len(candidates)
    tile_rows = tile_of(rows)
    steps = [(k, tile_rows) for k in range(0, rows, tile_rows)]

    def body(near_ref, block_ref, trail_ref, *refs):
        others, (out_ref, result, sems) = refs[:count], refs[-3:]

        def use(slot_b):
            def tile(at):
                return trail_ref[at, :] - slot_b(at)

            write_tiles(steps, tile, result, out_ref, pl.ds(half, half), sems)

        if first is None:
            with_slot_b(near_ref, members, block_ref, others, use)
        else:
            late = slots(near_ref, members)[1] != 0
            pl.when(late)(lambda: use(lambda at: dot(block_ref[at, first:], others[0][...])))
            pl.when(jnp.logical_not(late))(lambda: use(lambda at: 0.0))

    return call(
        body, shape(F32, *written.shape), (near, block, trail, *candidates, written),
        in_specs=[SMEM_SPEC] + [VMEM_SPEC] * (2 + count) + [ANY_SPEC], out_specs=ANY_SPEC,
        scratch=[VMEM((rows, half), F32), pltpu.SemaphoreType.DMA((len(steps),))],
        flops=2 * rows * rows * half, bytes_=rows * rows * 2 + rows * half * 10,
        aliases={3 + count: 0},
    )


def merge_all(message, first, rank):
    members = lax.axis_size("member")
    width = first["own"].shape[1] - rank if first else message.shape[1] - rank
    if not paired(members):
        others = around(message, "member")
        state = {"own": message, "others": others}
        first = first or state
        merged = merge_ring(state, first, rank, width)
        return state, merged
    down = mates(members)
    up = mates(members)
    mate = permute(message, down)
    pair = pack((message, mate))
    crossed = permute(pair, [(i, beside_pair(i, members)) for i in range(members)])
    state = {"own": message, "pair": pair, "crossed": crossed}
    first = first or state
    summed = merge_line(state, first, rank, width)
    handed = permute(summed, up)
    state["handed"] = handed
    return state, choose(summed, handed, width)


def merge_ring(state, first, rank, width):
    count = len(state["others"]) + 1

    def body(*refs):
        total = jnp.zeros((rank, width), F32)
        for coeff, carried in zip(refs[:count], refs[count:-1]):
            total = total + dot_tn(carried[:, width:], coeff[:, :width])
        refs[-1][...] = total.astype(BF16)

    args = (state["own"], *state["others"], first["own"], *first["others"])
    return call(
        body, shape(BF16, rank, width), args,
        flops=2 * rank * rank * width * count, bytes_=rank * width * 4 * count,
    )


def merge_line(state, first, rank, width):
    def body(pair_ref, crossed_ref, first_pair_ref, first_crossed_ref, out_ref):
        total = jnp.zeros((rank, width), F32)
        for coeffs, carried in ((pair_ref, first_pair_ref), (crossed_ref, first_crossed_ref)):
            for rows in (slice(0, rank), slice(rank, 2 * rank)):
                total = total + dot_tn(carried[rows, width:], coeffs[rows, :width])
        out_ref[:, :width] = total.astype(BF16)
        out_ref[:, width:] = crossed_ref[rank:, :width]

    return call(
        body, shape(BF16, rank, 2 * width),
        (state["pair"], state["crossed"], first["pair"], first["crossed"]),
        flops=8 * rank * rank * width, bytes_=rank * width * 16,
    )


def choose(summed, handed, width):
    members = lax.axis_size("member")

    def body(summed_ref, handed_ref, out_ref):
        end = at_end(lax.axis_index("member"), members)
        out_ref[...] = jnp.where(end, handed_ref[:, :width], summed_ref[:, :width])

    return call(
        body, shape(BF16, summed.shape[0], width), (summed, handed),
        bytes_=summed.shape[0] * width * 6,
    )


def coupled_arrays(state):
    if "others" in state:
        return tuple(state["others"])
    return state["pair"], state["crossed"], state["handed"]


def coupled_views(refs, rank, width):
    members = lax.axis_size("member")
    member = lax.axis_index("member")
    if not paired(members):
        return [(lax.rem(member + (members - 1 - k), members), ref[:, :width]) for k, ref in enumerate(refs)]
    pair_ref, crossed_ref, handed_ref = refs
    lower = member < members // 2
    far_end = jnp.where(lower, members - 1, 0)
    far_middle = jnp.where(lower, members // 2, members // 2 - 1)
    own_end = members - 1 - far_end
    end = at_end(member, members)
    from_far_end = jnp.where(end, handed_ref[:, width:], crossed_ref[rank:, :width])
    return [
        (jnp.where(end, far_middle, own_end), pair_ref[rank:, :width]),
        (far_middle, crossed_ref[:rank, :width]),
        (far_end, from_far_end),
    ]


def pack(blocks):
    rank, width = blocks[0].shape

    def body(*refs):
        for k, ref in enumerate(refs[:-1]):
            refs[-1][k * rank : (k + 1) * rank, :] = ref[...]

    return call(
        body, shape(BF16, rank * len(blocks), width), blocks,
        bytes_=rank * width * 4 * len(blocks),
    )


def inner_of(groups):
    return 2 if groups % 2 == 0 else 1


def all_merged(merged):
    groups = lax.axis_size("group")
    inner = inner_of(groups)
    moved = []
    for k in range(1, groups // inner):
        moved.append(cycle(merged, "group", k * inner))
    if inner == 1:
        return moved, None
    packed = pack((merged, *moved))
    beside = lax.ppermute(packed, "group", [(g, g + 1 - 2 * (g % 2)) for g in range(groups)])
    return moved, beside


def couple(near, couplings, transfer, cross, messages, merged, beside):
    rank = transfer.shape[0]
    width = merged[0].shape[1]
    members = lax.axis_size("member")
    groups = lax.axis_size("group")
    inner = inner_of(groups)
    packed = () if beside is None else (beside,)

    arrays = coupled_arrays(messages)
    count = len(arrays)

    def body(near_ref, couplings_ref, transfer_ref, cross_ref, *refs):
        coeffs, others, out_ref = refs[:count], refs[count:-1], refs[-1]
        group = lax.axis_index("group")
        crossed = jnp.zeros((rank, width), F32)
        for k in range(1, groups // inner):
            source = lax.rem(group + (groups - k * inner), groups)
            crossed = crossed + dot(cross_ref[source], others[k - 1][...])
        if packed:
            side = group + 1 - 2 * lax.rem(group, 2)
            for k in range(groups // inner):
                source = lax.rem(side + (groups - k * inner), groups)
                crossed = crossed + dot(cross_ref[source], others[-1][k * rank : (k + 1) * rank, :])
        within = dot(transfer_ref[...], crossed.astype(BF16))
        for source, coeff in coupled_views(coeffs, rank, width):
            far = (source != near_ref[0, 0]) & (source != near_ref[0, 1])
            within = within + jnp.where(far, 1.0, 0.0) * dot(couplings_ref[source], coeff)
        out_ref[...] = within.astype(BF16)

    args = (near, couplings, transfer, cross, *arrays, *merged, *packed)
    return call(
        body, shape(BF16, rank, width), args, scalars=1,
        flops=2 * rank * rank * width * (members + groups), bytes_=rank * width * 2 * (members + groups) * 2,
    )


def around(array, axis):
    moved = []
    for k in range(1, lax.axis_size(axis)):
        moved.append(cycle(array, axis, k))
    return moved


def shards(
    points,
    right_sides,
    leaf_order,
    near_leaves,
    bases,
    couplings,
    transfers,
    cross_couplings,
    low_bound,
    high_bound,
):
    transfer = transfers[0]
    couplings = couplings[0]
    cross = cross_couplings[0]
    near = near_leaves
    low, high = low_bound.reshape(1, 1), high_bound.reshape(1, 1)

    line = paired(lax.axis_size("member"))

    def moved(block):
        if not line:
            blocks = exchange(block)
            return blocks, blocks
        inner, outer = hop(block)
        return (outer, inner), (inner, across(inner))

    points_a, points_b = moved(points)
    block_a = near_block(0, near, points, points_a)
    block_b = near_block(1, near, points, points_b)
    lead, trail = start_rows(right_sides, leaf_order, low, high)
    ordered = order_rows(right_sides, leaf_order)
    message = start_message(lead, trail, bases, transfer)
    rank = transfer.shape[0]
    messages, merged = merge_all(message, None, rank)
    lead_a, lead_b = moved(lead)
    trail_a, trail_b = moved(trail)
    own_block, rest = self_first(points, ordered, lead, trail, low, high)
    merged, beside = all_merged(merged)
    rest = subtract_near(near, block_a, rest, lead_a, trail_a)
    coupled = couple(near, couplings, transfer, cross, messages, merged, beside)
    first_lead, lead, coeff = turn(0, near, block_b, rest, lead_b, bases, coupled, ordered, low, high)
    first_trail, trail, coeff = turn(
        1, near, block_b, rest, trail_b, bases, coupled, ordered, low, high, (coeff,))

    coeffs, merged = merge_all(coeff, messages, rank)
    lead_a, lead_b = moved(lead)
    if line:
        inner, outer = hop(trail)
        trail_a = (outer, inner)
        cut = 2 * trail.shape[0] // 3 if trail.shape[0] % 384 == 0 else trail.shape[0] // 2
        early = across(inner[:cut])
        late = across(inner[cut:])
    else:
        trail_a, trail_b = moved(trail)
    solution_rows, rest = self_second(own_block, lead, trail, first_lead, first_trail, ordered, low, high)
    merged, beside = all_merged(merged)
    rest = subtract_near(near, block_a, rest, lead_a, trail_a)
    coupled = couple(near, couplings, transfer, cross, coeffs, merged, beside)
    residual, rest = final_lead(near, block_b, rest, lead_b, bases, coupled)
    if line:
        rest = trail_part(near, block_b, rest, inner, early)
        residual = final_trail(near, block_b, rest, (late,), cut, residual)
    else:
        residual = final_trail(near, block_b, rest, trail_b, None, residual)
    return solution_rows, residual


def solution(mesh):
    return jax.shard_map(
        shards,
        mesh=mesh,
        in_specs=(
            P(("group", "member"), None),
            P(("group", "member"), None),
            P(("group", "member"), None),
            P(("group", "member"), None),
            P(("group", "member"), None),
            P(("group", "member"), None, None, None),
            P(("group", "member"), None, None),
            P("group", None, None, None),
            P(),
            P(),
        ),
        out_specs=(P(("group", "member"), None), P(("group", "member"), None)),
        check_vma=False,
    )
```
